32 devices in a mesh: group: 2 (over y), section: 4 (over z), tensor: 4 (over x, core).
Axes of the slice: x: 2, y: 2, z: 4, core: 2. Of those that a mesh axis runs over, the one named last changes fastest.
Arguments:
- inputs: bfloat16 [48, 4096], P('group', 'tensor'), parts along dimension 0, may hold values from -6 to 6
- gains: float32 [4, 4096], P('section'), may hold values from 0.5 to 1.5
- w_query: bfloat16 [4, 4096, 4096], P('section', None, 'tensor'), may hold values from -0.09375 to 0.09375
- w_key: bfloat16 [4, 4096, 1024], P('section', None, 'tensor'), may hold values from -0.09375 to 0.09375
- w_value: bfloat16 [4, 4096, 1024], P('section', None, 'tensor'), may hold values from -0.09375 to 0.09375
- w_out: bfloat16 [4, 4096, 4096], P('section', 'tensor'), may hold values from -0.375 to 0.375
- key_cache: bfloat16 [4, 48, 128, 1024], P('section', 'group', None, 'tensor'), parts along dimension 1, may hold values from -64 to 64
- value_cache: bfloat16 [4, 48, 128, 1024], P('section', 'group', None, 'tensor'), parts along dimension 1, may hold values from -6 to 6
- cache_lens: int32 [48], P('group'), parts along dimension 0, may hold values from 1 to 128, as said below
- exit_plan: int32 [48], P('group'), parts along dimension 0, may hold values from 1 to 4, as said below
Outputs:
- section_hidden: bfloat16 [4, 48, 4096], P('section', 'group', 'tensor'), parts along dimension 1
- new_keys: bfloat16 [4, 48, 1024], P('section', 'group', 'tensor'), parts along dimension 1
- new_values: bfloat16 [4, 48, 1024], P('section', 'group', 'tensor'), parts along dimension 1
The draws below stay inside these ranges and needn't reach their ends.
There are 2 independent parts, one for each index of `group`. The reference program is written for one: setup_inputs(seed, part) draws one part's arguments, and reference() takes and returns one part's arrays. A program takes and returns all parts, laid end to end along the dimension named above; an argument that names none is the same for every part. Nothing has to cross between parts.
Inputs may be any that keep to these rules, and one draw needn't show every extreme that they name: Cached slots 0 to cache_lens - 1 of a row are live; some row has exactly 128. `exit_plan`: some row runs all 4 layers in full.
All inputs are finite; a program needn't handle non-finite values.
Results may differ from the reference program's by a relative error of at most 0.022.
The reference program's roundings to bfloat16 on the way count: a program that leaves them out, or rounds other values in their place, can miss the bound.
Values may be sent and summed in bfloat16 or wider, within the bound.
A program may use at most 128 MiB of HBM per device.

```python
import math
import jax
import jax.numpy as jnp
from jax import lax

D = 4096
HEADS = 32
KV_HEADS = 8
HEAD_DIM = 128
ROWS = 24
CACHE_LEN = 128
LAYERS = 4


def draw_key_cache(key, part):
    standard = jnp.clip(jax.random.normal(jax.random.fold_in(key, 11), (LAYERS, ROWS, CACHE_LEN, KV_HEADS * HEAD_DIM), jnp.float32), -4.0, 4.0)
    return standard.astype(jnp.bfloat16)


def draw_cache_lens(key, part):
    lengths = jax.random.randint(jax.random.fold_in(key, 21), (ROWS,), 1, CACHE_LEN + 1)
    chosen = jax.random.randint(jax.random.fold_in(key, 22), (), 0, ROWS)
    return lengths.at[chosen].set(CACHE_LEN).astype(jnp.int32)


def draw_exit_plan(key, part):
    planned = jax.random.randint(jax.random.fold_in(key, 31), (ROWS,), 1, LAYERS + 1)
    chosen = jax.random.randint(jax.random.fold_in(key, 32), (), 0, ROWS)
    return planned.at[chosen].set(LAYERS).astype(jnp.int32)


def block_scale(key, extent, cuts, least, high):
    gain = 1.0
    for dim, blocks in cuts:
        steps = jax.random.uniform(jax.random.fold_in(jax.random.fold_in(key, 6), dim), (blocks,), jnp.float32, least / len(cuts), high / len(cuts))
        gain = gain * jnp.repeat(jnp.exp(steps), extent[dim] // blocks).reshape((-1,) + (1,) * (len(extent) - 1 - dim))
    return gain


def centred(stream_key, dims, scale, bound, split=(), kind=jnp.bfloat16):
    drawn = scale * jax.random.normal(stream_key, dims, jnp.float32)
    if split:
        drawn = drawn * block_scale(stream_key, dims, split, -0.22, 0.18)
    return jnp.clip(drawn, -bound, bound).astype(kind)


def setup_inputs(seed: int = 0, part: int = 0) -> dict:
    key_of = jax.random.split(jax.random.key(seed), 11)
    own_keys = jax.random.split(jax.random.fold_in(key_of[10], part), 11)
    inputs = centred(own_keys[0], (ROWS, D), 1.0, 6.0, ((1, 4),))
    gains = jnp.clip(1.0 + 0.1 * jax.random.normal(key_of[1], (LAYERS, D), jnp.float32), 0.5, 1.5)
    w_query = centred(key_of[2], (LAYERS, D, HEADS * HEAD_DIM), D ** -0.5, 0.09375, ((0, 4), (2, 4)))
    w_key = centred(key_of[3], (LAYERS, D, KV_HEADS * HEAD_DIM), D ** -0.5, 0.09375, ((0, 4), (2, 4)))
    w_value = centred(key_of[4], (LAYERS, D, KV_HEADS * HEAD_DIM), D ** -0.5, 0.09375, ((0, 4), (2, 4)))
    w_out = centred(key_of[5], (LAYERS, HEADS * HEAD_DIM, D), (HEADS * HEAD_DIM // 16) ** -0.5, 0.375, ((0, 4), (1, 4)))
    key_cache = draw_key_cache(jax.random.fold_in(jax.random.fold_in(key_of[10], part), 71), part)
    value_cache = centred(own_keys[7], (LAYERS, ROWS, CACHE_LEN, KV_HEADS * HEAD_DIM), 1.0, 6.0, ((0, 4), (3, 4)))
    cache_lens = draw_cache_lens(jax.random.fold_in(jax.random.fold_in(key_of[10], part), 71), part)
    exit_plan = draw_exit_plan(jax.random.fold_in(jax.random.fold_in(key_of[10], part), 71), part)
    return dict(inputs=inputs, gains=gains, w_query=w_query, w_key=w_key, w_value=w_value, w_out=w_out, key_cache=key_cache, value_cache=value_cache, cache_lens=cache_lens, exit_plan=exit_plan)


NORM_EPSILON = 1e-05
ROPE_BASE = 500000.0
MASKED_SCORE = -1e+30

def rotate(vectors, positions):
    half_dim = vectors.shape[-1] // 2
    frequency = ROPE_BASE ** (-(jnp.arange(half_dim, dtype=jnp.float32) * 2.0 / vectors.shape[-1]))
    angles = positions.astype(jnp.float32)[:, None, None] * frequency[None, None, :]
    cos_part = jnp.cos(angles)
    sin_part = jnp.sin(angles)
    lower_half = vectors[..., :half_dim]
    upper_half = vectors[..., half_dim:]
    return jnp.concatenate([lower_half * cos_part - upper_half * sin_part, upper_half * cos_part + lower_half * sin_part], axis=-1)

def reference(inputs, gains, w_query, w_key, w_value, w_out, key_cache, value_cache, cache_lens, exit_plan):
    per_kv = HEADS // KV_HEADS
    inv_root = 1.0 / math.sqrt(HEAD_DIM)
    visible = jnp.arange(CACHE_LEN)[None, :] < cache_lens[:, None]
    hidden = inputs
    hidden_list = []
    key_list = []
    value_list = []
    for depth_at in range(LAYERS):
        widened = hidden.astype(jnp.float32)
        normed = (widened * lax.rsqrt(lax.optimization_barrier(jnp.mean(widened * widened, axis=-1, keepdims=True)) + NORM_EPSILON) * gains[depth_at][None, :]).astype(jnp.bfloat16)
        queries = jnp.dot(normed, w_query[depth_at], preferred_element_type=jnp.float32).reshape(ROWS, HEADS, HEAD_DIM)
        queries = rotate(queries, cache_lens).astype(jnp.bfloat16).reshape(ROWS, KV_HEADS, per_kv, HEAD_DIM)
        key_new = jnp.dot(normed, w_key[depth_at], preferred_element_type=jnp.float32).reshape(ROWS, KV_HEADS, HEAD_DIM)
        key_new = rotate(key_new, cache_lens).astype(jnp.bfloat16)
        value_new = jnp.dot(normed, w_value[depth_at], preferred_element_type=jnp.float32).astype(jnp.bfloat16).reshape(ROWS, KV_HEADS, HEAD_DIM)
        keys_old = key_cache[depth_at].reshape(ROWS, CACHE_LEN, KV_HEADS, HEAD_DIM).astype(jnp.float32)
        values_old = value_cache[depth_at].reshape(ROWS, CACHE_LEN, KV_HEADS, HEAD_DIM).astype(jnp.float32)
        query_wide = queries.astype(jnp.float32)
        scores_old = jnp.einsum('rhgd,rlhd->rhgl', query_wide, keys_old) * inv_root
        scores_old = jnp.where(visible[:, None, None, :], scores_old, MASKED_SCORE)
        score_new = jnp.einsum('rhgd,rhd->rhg', query_wide, key_new.astype(jnp.float32)) * inv_root
        highest = jnp.maximum(lax.optimization_barrier(jnp.max(scores_old, axis=-1)), score_new)
        weight_old = jnp.exp(scores_old - highest[..., None])
        weight_new = jnp.exp(score_new - highest)
        denominator = lax.optimization_barrier(jnp.sum(weight_old, axis=-1)) + weight_new
        weight_old = (weight_old / denominator[..., None]).astype(jnp.bfloat16)
        weight_new = (weight_new / denominator).astype(jnp.bfloat16)
        attended = jnp.einsum('rhgl,rlhd->rhgd', weight_old.astype(jnp.float32), values_old)
        attended = attended + weight_new.astype(jnp.float32)[..., None] * value_new.astype(jnp.float32)[:, :, None, :]
        attended = attended.astype(jnp.bfloat16).reshape(ROWS, HEADS * HEAD_DIM)
        update = jnp.dot(attended, w_out[depth_at], preferred_element_type=jnp.float32)
        running = (depth_at < exit_plan).astype(jnp.float32)[:, None]
        hidden = (widened + running * update).astype(jnp.bfloat16)
        hidden_list.append(hidden)
        key_list.append(key_new.reshape(ROWS, KV_HEADS * HEAD_DIM))
        value_list.append(value_new.reshape(ROWS, KV_HEADS * HEAD_DIM))
    return (jnp.stack(hidden_list), jnp.stack(key_list), jnp.stack(value_list))
```

```python
import functools
import math

import jax
import jax.numpy as jnp
from jax import lax
from jax.experimental import pallas as pl
from jax.experimental.pallas import tpu as pltpu
from jax.sharding import PartitionSpec as P

HEAD_DIM = 128
NORM_EPSILON = 1e-05
ROPE_BASE = 500000.0
MASKED_SCORE = -1e30
MESH = pl.DeviceIdType.MESH


def split_rows(rows):
    first = -(-rows // 2 // 16) * 16
    cuts = [(first, rows - first), (0, first)]
    return [cut for cut in cuts if cut[1] > 0]


def relay_kernel(
    sections, tensors, groups_per_kv, batches,
    lens_ref, plan_ref, inputs_ref, gains_ref, wq_ref, wk_ref, wv_ref, wo_ref, kc_ref, vc_ref,
    out_hidden, out_keys, out_values,
    wq, wk, wv, wo, kc, vc, gain, own, normed,
    pos, running, mask, queries, scores, score_new, values_new, attended,
    load_sem, stages,
):
    rows, width = own.shape
    chips = tensors // 2
    kv_local = wk.shape[1] // HEAD_DIM
    heads = kv_local * groups_per_kv
    slot = queries.shape[0] // rows
    slots = kc.shape[1]
    section = lax.axis_index("section")
    me = lax.axis_index("tensor")
    chip = me // 2
    core = lax.rem(me, 2)
    sibling = {"tensor": 2 * chip + 1 - core}

    def load(source, target, index):
        return pltpu.make_async_copy(source, target, load_sem.at[index])

    def remote(source, target, send_sem, recv_sem, device):
        return pltpu.make_async_remote_copy(
            src_ref=source, dst_ref=target, send_sem=send_sem, recv_sem=recv_sem,
            device_id=device, device_id_type=MESH,
        )

    loads = dict(
        gain=load(gains_ref, gain, 0),
        wk=load(wk_ref.at[0], wk, 1),
        wv=load(wv_ref.at[0], wv, 2),
        wq=load(wq_ref.at[0], wq, 3),
        kc=load(kc_ref.at[0], kc, 4),
        vc=load(vc_ref.at[0], vc, 5),
        wo=load(wo_ref.at[0], wo, 6),
    )
    own_entering = load(inputs_ref, own, 7)

    @pl.when(section == 0)
    def _():
        own_entering.start()

    for name in ("gain", "wk", "wv", "wq", "kc"):
        loads[name].start()

    @pl.when(section > 0)
    def _():
        for name in ("vc", "wo"):
            loads[name].start()

    barrier = pltpu.get_barrier_semaphore()

    def greet(device):
        pl.semaphore_signal(barrier, inc=1, device_id=device, device_id_type=MESH)

    for off in range(1, tensors):
        greet({"tensor": lax.rem(me + off, tensors)})

    @pl.when(section > 0)
    def _():
        for other in range(chips):
            greet({"section": section - 1, "tensor": 2 * other + core})

    @pl.when(section < sections - 1)
    def _():
        for other in range(chips):
            greet({"section": section + 1, "tensor": 2 * other + core})

    pl.semaphore_wait(
        barrier,
        (tensors - 1)
        + chips * (section > 0).astype(jnp.int32)
        + chips * (section < sections - 1).astype(jnp.int32),
    )

    def entering(stage, off):
        return remote(
            stage["hid"].at[core, chip], stage["hid"].at[core, chip],
            stage["enter_send"].at[off], stage["enter_recv"].at[core, chip],
            {"tensor": lax.rem(me + off, tensors)},
        )

    def swap_half(stage, half, at):
        hid = stage["hid"]
        return remote(
            hid.at[half, at], hid.at[half, at], stage["half_send"].at[at],
            stage["half_recv"].at[at], sibling,
        )

    def send_sum(stage, target, at):
        return remote(
            stage["chip_sum"].at[at], stage["sums_in"].at[chip, at],
            stage["sums_send"].at[target, at], stage["sums_recv"].at[chip, at],
            {"section": section + 1, "tensor": 2 * target + core},
        )

    def send_before(stage):
        return remote(
            stage["hid"].at[core], stage["before"], stage["before_send"].at[0],
            stage["before_recv"].at[0], {"section": section + 1},
        )

    def send_part(stage, at):
        return remote(
            stage["part"].at[at], stage["part_in"].at[at], stage["part_send"].at[at],
            stage["part_recv"].at[at], sibling,
        )

    def send_piece(stage, at):
        return remote(
            stage["chip_sum"].at[at], stage["piece_in"].at[chip], stage["piece_send"].at[at],
            stage["piece_recv"].at[chip], {"tensor": 2 * at + core},
        )

    @pl.when(section == 0)
    def _():
        own_entering.wait()
        for (first, count), stage in zip(batches, stages):
            stage["hid"][core, chip] = own[first : first + count, :]
            for off in range(1, tensors):
                entering(stage, off).start()
        for name in ("vc", "wo"):
            loads[name].start()

    lane = lax.broadcasted_iota(jnp.int32, (slot, slots), 1)
    for row in range(rows):
        length = lens_ref[row]
        pos[row : row + 1, :] = jnp.full((1, HEAD_DIM), length, jnp.int32).astype(jnp.float32)
        planned = jnp.full((1, HEAD_DIM), plan_ref[row], jnp.int32)
        running[0, row : row + 1, :] = (planned > section).astype(jnp.float32)
        running[1, row : row + 1, :] = (planned > section - 1).astype(jnp.float32)
        mask[row * slot : (row + 1) * slot, :] = (lane < length).astype(jnp.float32)
    half_lane = lax.broadcasted_iota(jnp.int32, (rows, HEAD_DIM), 1)
    half = HEAD_DIM // 2
    step_at = jnp.where(half_lane < half, half_lane, half_lane - half).astype(jnp.float32)
    frequency = jnp.exp(step_at * (-2.0 * math.log(ROPE_BASE) / HEAD_DIM))
    angles = pos[...] * frequency
    cos_part = jnp.cos(angles)
    sin_part = jnp.sin(angles)
    sin_part = jnp.where(half_lane < half, -sin_part, sin_part)
    if heads < slot:
        queries[...] = jnp.zeros_like(queries)
        score_new[...] = jnp.zeros_like(score_new)
        values_new[...] = jnp.zeros_like(values_new)

    def receive(index):
        (first, count), stage = batches[index], stages[index]
        hid = stage["hid"]

        @pl.when(section == 0)
        def _():
            for off in range(1, tensors):
                other = lax.rem(me + off, tensors)
                at = (lax.rem(other, 2), other // 2)
                remote(
                    hid.at[at], hid.at[at], stage["enter_send"].at[off],
                    stage["enter_recv"].at[at], sibling,
                ).wait_recv()

        @pl.when(section > 0)
        def _():
            before, sums_in = stage["before"], stage["sums_in"]
            remote(
                before, before, stage["before_send"].at[0], stage["before_recv"].at[0],
                {"section": section - 1},
            ).wait_recv()
            for at in range(chips):
                total = jnp.zeros((count, width), jnp.float32)
                for source in range(chips):
                    remote(
                        sums_in.at[source, at], sums_in.at[source, at],
                        stage["sums_send"].at[source, at], stage["sums_recv"].at[source, at],
                        {"section": section - 1},
                    ).wait_recv()
                    total = total + sums_in[source, at].astype(jnp.float32)
                wide = before[at].astype(jnp.float32)
                on = running[1, first : first + count, :1]
                hid[core, at] = (wide + on * total).astype(jnp.bfloat16)
                swap_half(stage, core, at).start()
            for at in range(chips):
                swap_half(stage, 1 - core, at).wait_recv()

        @pl.when(section < sections - 1)
        def _():
            send_before(stage).start()

    inv_root = 1.0 / math.sqrt(HEAD_DIM)
    head_of = lax.broadcasted_iota(jnp.int32, (slot, HEAD_DIM), 0) // groups_per_kv

    def compute(index):
        (first, count), stage = batches[index], stages[index]
        hid = stage["hid"]
        span = slice(first, first + count)
        cos_here, sin_here = cos_part[span, :], sin_part[span, :]

        def rotate(vectors):
            return vectors * cos_here + pltpu.roll(vectors, half, 1) * sin_here

        if index == 0:
            loads["gain"].wait()
        squares = jnp.zeros((count, 1), jnp.float32)
        for source in range(tensors):
            wide = hid[source % 2, source // 2].astype(jnp.float32)
            squares = squares + jnp.sum(wide * wide, axis=-1, keepdims=True)
        scale = lax.rsqrt(squares / (tensors * width) + NORM_EPSILON)
        for source in range(tensors):
            at = slice(source * width, (source + 1) * width)
            wide = hid[source % 2, source // 2].astype(jnp.float32)
            normed[span, at] = (wide * scale * gain[:, at]).astype(jnp.bfloat16)

        entered = normed[span, :]
        if index == 0:
            loads["wk"].wait()
        key_new = jnp.dot(entered, wk[...], preferred_element_type=jnp.float32)
        if index == 0:
            loads["wv"].wait()
        value_new = jnp.dot(entered, wv[...], preferred_element_type=jnp.float32)
        value_new = value_new.astype(jnp.bfloat16)
        out_values[0, span, :] = value_new
        keys = []
        values = []
        for kv in range(kv_local):
            at = slice(kv * HEAD_DIM, (kv + 1) * HEAD_DIM)
            rotated = rotate(key_new[:, at]).astype(jnp.bfloat16)
            out_keys[0, span, at] = rotated
            keys.append(rotated.astype(jnp.float32))
            values.append(value_new[:, at].astype(jnp.float32))

        if index == 0:
            loads["wq"].wait()
        tile = min(256, heads * HEAD_DIM)
        for start in range(0, heads * HEAD_DIM, tile):
            product = jnp.dot(
                entered, wq[:, start : start + tile], preferred_element_type=jnp.float32
            )
            for inner in range(tile // HEAD_DIM):
                head = start // HEAD_DIM + inner
                kv = head // groups_per_kv
                query = rotate(product[:, inner * HEAD_DIM : (inner + 1) * HEAD_DIM])
                query = query.astype(jnp.bfloat16).astype(jnp.float32)
                at = pl.ds(first * slot + head, count, stride=slot)
                queries[at, :] = query
                score = jnp.sum(query * keys[kv], axis=-1, keepdims=True) * inv_root
                score_new[at, :] = jnp.broadcast_to(score, (count, HEAD_DIM))
                values_new[at, :] = values[kv]

        if index == 0:
            loads["kc"].wait()
        for row in range(first, first + count):
            at = slice(row * slot, (row + 1) * slot)
            query = queries[at, :]
            spread = jnp.concatenate(
                [jnp.where(head_of == kv, query, 0.0) for kv in range(kv_local)], axis=1
            ).astype(jnp.bfloat16)
            scores[at, :] = lax.dot_general(
                spread, kc[row], (((1,), (1,)), ((), ())), preferred_element_type=jnp.float32
            )

        lines = slice(first * slot, (first + count) * slot)
        old = jnp.where(mask[lines, :] > 0.0, scores[lines, :] * inv_root, MASKED_SCORE)
        new = score_new[lines, :1]
        highest = jnp.maximum(jnp.max(old, axis=-1, keepdims=True), new)
        weight_old = jnp.exp(old - highest)
        weight_new = jnp.exp(new - highest)
        denominator = jnp.sum(weight_old, axis=-1, keepdims=True) + weight_new
        scores[lines, :] = weight_old / denominator
        weight_new = (weight_new / denominator).astype(jnp.bfloat16).astype(jnp.float32)
        values_new[lines, :] = values_new[lines, :] * weight_new

        if index == 0:
            loads["vc"].wait()
        for row in range(first, first + count):
            at = slice(row * slot, (row + 1) * slot)
            mixed = jnp.dot(
                scores[at, :].astype(jnp.bfloat16), vc[row], preferred_element_type=jnp.float32
            )
            taken = mixed[:, :HEAD_DIM]
            for kv in range(1, kv_local):
                taken = jnp.where(
                    head_of == kv, mixed[:, kv * HEAD_DIM : (kv + 1) * HEAD_DIM], taken
                )
            attended[at, :] = taken + values_new[at, :]

        flat = jnp.concatenate(
            [
                attended[pl.ds(first * slot + head, count, stride=slot), :].astype(jnp.bfloat16)
                for head in range(heads)
            ],
            axis=1,
        )

        if index == 0:
            loads["wo"].wait()

        def project(half, at):
            start = (2 * at + half) * width
            columns = pl.ds(pl.multiple_of(start, width), width)
            return jnp.dot(flat, wo[:, columns], preferred_element_type=jnp.float32)

        part, part_in, chip_sum = stage["part"], stage["part_in"], stage["chip_sum"]
        for at in range(chips):
            part[at] = project(1 - core, at).astype(jnp.bfloat16)
            send_part(stage, at).start()
        for at in range(chips):
            mine = project(core, at)
            send_part(stage, at).wait_recv()
            chip_sum[at] = (mine + part_in[at].astype(jnp.float32)).astype(jnp.bfloat16)

            @pl.when(section < sections - 1)
            def _():
                for target in range(chips):
                    send_sum(stage, target, at).start()

            @pl.when(chip != at)
            def _():
                send_piece(stage, at).start()

    def finish(index):
        (first, count), stage = batches[index], stages[index]
        piece_in, chip_sum = stage["piece_in"], stage["chip_sum"]
        piece_in[chip] = chip_sum[chip]
        total = jnp.zeros((count, width), jnp.float32)
        for source in range(chips):
            @pl.when(chip != source)
            def _():
                remote(
                    piece_in.at[source], piece_in.at[source], stage["piece_send"].at[source],
                    stage["piece_recv"].at[source], sibling,
                ).wait_recv()

            total = total + piece_in[source].astype(jnp.float32)
        wide = stage["hid"][core, chip].astype(jnp.float32)
        on = running[0, first : first + count, :1]
        out_hidden[0, first : first + count, :] = (wide + on * total).astype(jnp.bfloat16)

    for index in range(len(batches)):
        receive(index)
        compute(index)
    for index in range(len(batches)):
        finish(index)

    for stage in stages:
        @pl.when(section == 0)
        def _():
            for off in range(1, tensors):
                entering(stage, off).wait_send()

        @pl.when(section > 0)
        def _():
            for at in range(chips):
                swap_half(stage, core, at).wait_send()

        @pl.when(section < sections - 1)
        def _():
            send_before(stage).wait_send()
            for at in range(chips):
                for target in range(chips):
                    send_sum(stage, target, at).wait_send()

        for at in range(chips):
            send_part(stage, at).wait_send()

            @pl.when(chip != at)
            def _():
                send_piece(stage, at).wait_send()


def emit_kernel(hidden_ref, keys_ref, values_ref, out_hidden, out_keys, out_values):
    out_hidden[...] = hidden_ref[...]
    out_keys[...] = keys_ref[...]
    out_values[...] = values_ref[...]


def solution(mesh):
    sections = mesh.shape["section"]
    tensors = mesh.shape["tensor"]
    chips = tensors // 2

    def per_device(
        inputs, gains, w_query, w_key, w_value, w_out, key_cache, value_cache, cache_lens, exit_plan
    ):
        rows, width = inputs.shape
        features = gains.shape[1]
        query_width = w_query.shape[2]
        kv_width = w_key.shape[2]
        heads = query_width // HEAD_DIM
        groups_per_kv = query_width // kv_width
        slot = -(-heads // 8) * 8
        slots = key_cache.shape[2]
        any_spec = pl.BlockSpec(memory_space=pl.ANY)
        smem_spec = pl.BlockSpec(memory_space=pltpu.SMEM)
        vmem_spec = pl.BlockSpec(memory_space=pltpu.VMEM)
        bf16, f32 = jnp.bfloat16, jnp.float32
        batches = split_rows(rows)

        def stage_scratch(count):
            def blocks(*shape):
                return pltpu.VMEM((*shape, count, width), bf16)

            def sems(*shape):
                return pltpu.SemaphoreType.DMA(shape)

            return dict(
                hid=blocks(2, chips), before=blocks(chips), part=blocks(chips),
                part_in=blocks(chips), chip_sum=blocks(chips), sums_in=blocks(chips, chips),
                piece_in=blocks(chips), enter_send=sems(tensors), enter_recv=sems(2, chips),
                half_send=sems(chips), half_recv=sems(chips), before_send=sems(1),
                before_recv=sems(1), part_send=sems(chips), part_recv=sems(chips),
                sums_send=sems(chips, chips), sums_recv=sems(chips, chips),
                piece_send=sems(chips), piece_recv=sems(chips),
            )

        results = pl.pallas_call(
            functools.partial(relay_kernel, sections, tensors, groups_per_kv, batches),
            out_shape=(
                jax.ShapeDtypeStruct((1, rows, width), bf16),
                jax.ShapeDtypeStruct((1, rows, kv_width), bf16),
                jax.ShapeDtypeStruct((1, rows, kv_width), bf16),
            ),
            in_specs=[smem_spec] * 2 + [any_spec] * 8,
            out_specs=(vmem_spec,) * 3,
            scratch_shapes=[
                pltpu.VMEM((features, query_width), bf16),
                pltpu.VMEM((features, kv_width), bf16),
                pltpu.VMEM((features, kv_width), bf16),
                pltpu.VMEM((query_width, features), bf16),
                pltpu.VMEM((rows, slots, kv_width), bf16),
                pltpu.VMEM((rows, slots, kv_width), bf16),
                pltpu.VMEM((1, features), f32),
                pltpu.VMEM((rows, width), bf16),
                pltpu.VMEM((rows, features), bf16),
                pltpu.VMEM((rows, HEAD_DIM), f32),
                pltpu.VMEM((2, rows, HEAD_DIM), f32),
                pltpu.VMEM((rows * slot, slots), f32),
                pltpu.VMEM((rows * slot, HEAD_DIM), f32),
                pltpu.VMEM((rows * slot, slots), f32),
                pltpu.VMEM((rows * slot, HEAD_DIM), f32),
                pltpu.VMEM((rows * slot, HEAD_DIM), f32),
                pltpu.VMEM((rows * slot, HEAD_DIM), f32),
                pltpu.SemaphoreType.DMA((8,)),
                tuple(stage_scratch(count) for _, count in batches),
            ],
            compiler_params=pltpu.CompilerParams(
                collective_id=0, has_side_effects=True, vmem_limit_bytes=63 * 1024 * 1024
            ),
            name="relay",
        )(
            cache_lens, exit_plan, inputs, gains, w_query, w_key, w_value, w_out,
            key_cache, value_cache,
        )
        return pl.pallas_call(
            emit_kernel,
            out_shape=tuple(jax.ShapeDtypeStruct(r.shape, r.dtype) for r in results),
            in_specs=[vmem_spec] * 3,
            out_specs=(vmem_spec,) * 3,
            name="emit",
        )(*results)

    return jax.shard_map(
        per_device,
        mesh=mesh,
        in_specs=(
            P("group", "tensor"),
            P("section", None),
            P("section", None, "tensor"),
            P("section", None, "tensor"),
            P("section", None, "tensor"),
            P("section", "tensor", None),
            P("section", "group", None, "tensor"),
            P("section", "group", None, "tensor"),
            P("group"),
            P("group"),
        ),
        out_specs=(
            P("section", "group", "tensor"),
            P("section", "group", "tensor"),
            P("section", "group", "tensor"),
        ),
        check_vma=False,
    )
```

```python
import functools
import math

import jax
import jax.numpy as jnp
from jax import lax
from jax.experimental import pallas as pl
from jax.experimental.pallas import tpu as pltpu
from jax.sharding import PartitionSpec as P

HEAD_DIM = 128
NORM_EPSILON = 1e-05
ROPE_BASE = 500000.0
MASKED_SCORE = -1e30
MESH = pl.DeviceIdType.MESH


def split_rows(rows):
    first = -(-rows // 2 // 16) * 16
    cuts = [(first, rows - first), (0, first)]
    return [cut for cut in cuts if cut[1] > 0]


def relay_kernel(
    sections, tensors, groups_per_kv, batches,
    lens_ref, plan_ref, inputs_ref, gains_ref, wq_ref, wk_ref, wv_ref, wo_ref, kc_ref, vc_ref,
    out_hidden, out_keys, out_values,
    wq, wk, wv, wo, kc, vc, gain, own, normed,
    pos, running, mask, queries, scores, score_new, values_new, attended,
    lens, plan, load_sem, stages,
):
    rows, width = own.shape
    chips = tensors // 2
    kv_local = wk.shape[1] // HEAD_DIM
    heads = kv_local * groups_per_kv
    slot = queries.shape[0] // rows
    slots = kc.shape[1]
    section = lax.axis_index("section")
    me = lax.axis_index("tensor")
    chip = me // 2
    core = lax.rem(me, 2)
    sibling = {"tensor": 2 * chip + 1 - core}

    def load(source, target, index):
        return pltpu.make_async_copy(source, target, load_sem.at[index])

    def remote(source, target, send_sem, recv_sem, device):
        return pltpu.make_async_remote_copy(
            src_ref=source, dst_ref=target, send_sem=send_sem, recv_sem=recv_sem,
            device_id=device, device_id_type=MESH,
        )

    loads = dict(
        gain=load(gains_ref, gain, 0),
        wk=load(wk_ref.at[0], wk, 1),
        wv=load(wv_ref.at[0], wv, 2),
        wq=load(wq_ref.at[0], wq, 3),
        kc=load(kc_ref.at[0], kc, 4),
        vc=load(vc_ref.at[0], vc, 5),
        wo=load(wo_ref.at[0], wo, 6),
        lens=load(lens_ref, lens, 8),
        plan=load(plan_ref, plan, 9),
    )
    own_entering = load(inputs_ref, own, 7)

    @pl.when(section == 0)
    def _():
        own_entering.start()

    for name in ("lens", "plan", "gain", "wk", "wv", "wq", "kc"):
        loads[name].start()

    @pl.when(section > 0)
    def _():
        for name in ("vc", "wo"):
            loads[name].start()

    barrier = pltpu.get_barrier_semaphore()

    def greet(device):
        pl.semaphore_signal(barrier, inc=1, device_id=device, device_id_type=MESH)

    for off in range(1, tensors):
        greet({"tensor": lax.rem(me + off, tensors)})

    @pl.when(section > 0)
    def _():
        for other in range(chips):
            greet({"section": section - 1, "tensor": 2 * other + core})

    @pl.when(section < sections - 1)
    def _():
        for other in range(chips):
            greet({"section": section + 1, "tensor": 2 * other + core})

    pl.semaphore_wait(
        barrier,
        (tensors - 1)
        + chips * (section > 0).astype(jnp.int32)
        + chips * (section < sections - 1).astype(jnp.int32),
    )

    def entering(stage, off):
        return remote(
            stage["hid"].at[core, chip], stage["hid"].at[core, chip],
            stage["enter_send"].at[off], stage["enter_recv"].at[core, chip],
            {"tensor": lax.rem(me + off, tensors)},
        )

    def swap_half(stage, half, at):
        hid = stage["hid"]
        return remote(
            hid.at[half, at], hid.at[half, at], stage["half_send"].at[at],
            stage["half_recv"].at[at], sibling,
        )

    def send_sum(stage, target, at):
        return remote(
            stage["chip_sum"].at[at], stage["sums_in"].at[chip, at],
            stage["sums_send"].at[target, at], stage["sums_recv"].at[chip, at],
            {"section": section + 1, "tensor": 2 * target + core},
        )

    def send_before(stage):
        return remote(
            stage["hid"].at[core], stage["before"], stage["before_send"].at[0],
            stage["before_recv"].at[0], {"section": section + 1},
        )

    def send_part(stage, at):
        return remote(
            stage["part"].at[at], stage["part_in"].at[at], stage["part_send"].at[at],
            stage["part_recv"].at[at], sibling,
        )

    def send_piece(stage, at):
        return remote(
            stage["chip_sum"].at[at], stage["piece_in"].at[chip], stage["piece_send"].at[at],
            stage["piece_recv"].at[chip], {"tensor": 2 * at + core},
        )

    @pl.when(section == 0)
    def _():
        own_entering.wait()
        for (first, count), stage in zip(batches, stages):
            stage["hid"][core, chip] = own[first : first + count, :]
            for off in range(1, tensors):
                entering(stage, off).start()
        for name in ("vc", "wo"):
            loads[name].start()

    lane = lax.broadcasted_iota(jnp.int32, (slot, slots), 1)
    for name in ("lens", "plan"):
        loads[name].wait()
    for row in range(rows):
        length = lens[row]
        pos[row : row + 1, :] = jnp.full((1, HEAD_DIM), length, jnp.int32).astype(jnp.float32)
        planned = jnp.full((1, HEAD_DIM), plan[row], jnp.int32)
        running[0, row : row + 1, :] = (planned > section).astype(jnp.float32)
        running[1, row : row + 1, :] = (planned > section - 1).astype(jnp.float32)
        mask[row * slot : (row + 1) * slot, :] = (lane < length).astype(jnp.float32)
    half_lane = lax.broadcasted_iota(jnp.int32, (rows, HEAD_DIM), 1)
    half = HEAD_DIM // 2
    step_at = jnp.where(half_lane < half, half_lane, half_lane - half).astype(jnp.float32)
    frequency = jnp.exp(step_at * (-2.0 * math.log(ROPE_BASE) / HEAD_DIM))
    angles = pos[...] * frequency
    cos_part = jnp.cos(angles)
    sin_part = jnp.sin(angles)
    sin_part = jnp.where(half_lane < half, -sin_part, sin_part)
    if heads < slot:
        queries[...] = jnp.zeros_like(queries)
        score_new[...] = jnp.zeros_like(score_new)
        values_new[...] = jnp.zeros_like(values_new)

    def receive(index):
        (first, count), stage = batches[index], stages[index]
        hid = stage["hid"]

        @pl.when(section == 0)
        def _():
            for off in range(1, tensors):
                other = lax.rem(me + off, tensors)
                at = (lax.rem(other, 2), other // 2)
                remote(
                    hid.at[at], hid.at[at], stage["enter_send"].at[off],
                    stage["enter_recv"].at[at], sibling,
                ).wait_recv()

        @pl.when(section > 0)
        def _():
            before, sums_in = stage["before"], stage["sums_in"]
            remote(
                before, before, stage["before_send"].at[0], stage["before_recv"].at[0],
                {"section": section - 1},
            ).wait_recv()
            for at in range(chips):
                total = jnp.zeros((count, width), jnp.float32)
                for source in range(chips):
                    remote(
                        sums_in.at[source, at], sums_in.at[source, at],
                        stage["sums_send"].at[source, at], stage["sums_recv"].at[source, at],
                        {"section": section - 1},
                    ).wait_recv()
                    total = total + sums_in[source, at].astype(jnp.float32)
                wide = before[at].astype(jnp.float32)
                on = running[1, first : first + count, :1]
                hid[core, at] = (wide + on * total).astype(jnp.bfloat16)
                swap_half(stage, core, at).start()
            for at in range(chips):
                swap_half(stage, 1 - core, at).wait_recv()

        @pl.when(section < sections - 1)
        def _():
            send_before(stage).start()

    inv_root = 1.0 / math.sqrt(HEAD_DIM)
    head_of = lax.broadcasted_iota(jnp.int32, (slot, HEAD_DIM), 0) // groups_per_kv

    def compute(index):
        (first, count), stage = batches[index], stages[index]
        hid = stage["hid"]
        span = slice(first, first + count)
        cos_here, sin_here = cos_part[span, :], sin_part[span, :]

        def rotate(vectors):
            return vectors * cos_here + pltpu.roll(vectors, half, 1) * sin_here

        if index == 0:
            loads["gain"].wait()
        squares = jnp.zeros((count, 1), jnp.float32)
        for source in range(tensors):
            wide = hid[source % 2, source // 2].astype(jnp.float32)
            squares = squares + jnp.sum(wide * wide, axis=-1, keepdims=True)
        scale = lax.rsqrt(squares / (tensors * width) + NORM_EPSILON)
        for source in range(tensors):
            at = slice(source * width, (source + 1) * width)
            wide = hid[source % 2, source // 2].astype(jnp.float32)
            normed[span, at] = (wide * scale * gain[:, at]).astype(jnp.bfloat16)

        entered = normed[span, :]
        if index == 0:
            loads["wk"].wait()
        key_new = jnp.dot(entered, wk[...], preferred_element_type=jnp.float32)
        if index == 0:
            loads["wv"].wait()
        value_new = jnp.dot(entered, wv[...], preferred_element_type=jnp.float32)
        value_new = value_new.astype(jnp.bfloat16)
        out_values[0, span, :] = value_new
        keys = []
        values = []
        for kv in range(kv_local):
            at = slice(kv * HEAD_DIM, (kv + 1) * HEAD_DIM)
            rotated = rotate(key_new[:, at]).astype(jnp.bfloat16)
            out_keys[0, span, at] = rotated
            keys.append(rotated.astype(jnp.float32))
            values.append(value_new[:, at].astype(jnp.float32))

        if index == 0:
            loads["wq"].wait()
        tile = min(256, heads * HEAD_DIM)
        for start in range(0, heads * HEAD_DIM, tile):
            product = jnp.dot(
                entered, wq[:, start : start + tile], preferred_element_type=jnp.float32
            )
            for inner in range(tile // HEAD_DIM):
                head = start // HEAD_DIM + inner
                kv = head // groups_per_kv
                query = rotate(product[:, inner * HEAD_DIM : (inner + 1) * HEAD_DIM])
                query = query.astype(jnp.bfloat16).astype(jnp.float32)
                at = pl.ds(first * slot + head, count, stride=slot)
                queries[at, :] = query
                score = jnp.sum(query * keys[kv], axis=-1, keepdims=True) * inv_root
                score_new[at, :] = jnp.broadcast_to(score, (count, HEAD_DIM))
                values_new[at, :] = values[kv]

        if index == 0:
            loads["kc"].wait()
        for row in range(first, first + count):
            at = slice(row * slot, (row + 1) * slot)
            query = queries[at, :]
            spread = jnp.concatenate(
                [jnp.where(head_of == kv, query, 0.0) for kv in range(kv_local)], axis=1
            ).astype(jnp.bfloat16)
            scores[at, :] = lax.dot_general(
                spread, kc[row], (((1,), (1,)), ((), ())), preferred_element_type=jnp.float32
            )

        lines = slice(first * slot, (first + count) * slot)
        old = jnp.where(mask[lines, :] > 0.0, scores[lines, :] * inv_root, MASKED_SCORE)
        new = score_new[lines, :1]
        highest = jnp.maximum(jnp.max(old, axis=-1, keepdims=True), new)
        weight_old = jnp.exp(old - highest)
        weight_new = jnp.exp(new - highest)
        denominator = jnp.sum(weight_old, axis=-1, keepdims=True) + weight_new
        scores[lines, :] = weight_old / denominator
        weight_new = (weight_new / denominator).astype(jnp.bfloat16).astype(jnp.float32)
        values_new[lines, :] = values_new[lines, :] * weight_new

        if index == 0:
            loads["vc"].wait()
        for row in range(first, first + count):
            at = slice(row * slot, (row + 1) * slot)
            mixed = jnp.dot(
                scores[at, :].astype(jnp.bfloat16), vc[row], preferred_element_type=jnp.float32
            )
            taken = mixed[:, :HEAD_DIM]
            for kv in range(1, kv_local):
                taken = jnp.where(
                    head_of == kv, mixed[:, kv * HEAD_DIM : (kv + 1) * HEAD_DIM], taken
                )
            attended[at, :] = taken + values_new[at, :]

        flat = jnp.concatenate(
            [
                attended[pl.ds(first * slot + head, count, stride=slot), :].astype(jnp.bfloat16)
                for head in range(heads)
            ],
            axis=1,
        )

        if index == 0:
            loads["wo"].wait()

        def project(half, at):
            start = (2 * at + half) * width
            columns = pl.ds(pl.multiple_of(start, width), width)
            return jnp.dot(flat, wo[:, columns], preferred_element_type=jnp.float32)

        part, part_in, chip_sum = stage["part"], stage["part_in"], stage["chip_sum"]
        for at in range(chips):
            part[at] = project(1 - core, at).astype(jnp.bfloat16)
            send_part(stage, at).start()
        for at in range(chips):
            mine = project(core, at)
            send_part(stage, at).wait_recv()
            chip_sum[at] = (mine + part_in[at].astype(jnp.float32)).astype(jnp.bfloat16)

            @pl.when(section < sections - 1)
            def _():
                for target in range(chips):
                    send_sum(stage, target, at).start()

            @pl.when(chip != at)
            def _():
                send_piece(stage, at).start()

    def finish(index):
        (first, count), stage = batches[index], stages[index]
        piece_in, chip_sum = stage["piece_in"], stage["chip_sum"]
        piece_in[chip] = chip_sum[chip]
        total = jnp.zeros((count, width), jnp.float32)
        for source in range(chips):
            @pl.when(chip != source)
            def _():
                remote(
                    piece_in.at[source], piece_in.at[source], stage["piece_send"].at[source],
                    stage["piece_recv"].at[source], sibling,
                ).wait_recv()

            total = total + piece_in[source].astype(jnp.float32)
        wide = stage["hid"][core, chip].astype(jnp.float32)
        on = running[0, first : first + count, :1]
        out_hidden[0, first : first + count, :] = (wide + on * total).astype(jnp.bfloat16)

    for index in range(len(batches)):
        receive(index)
        compute(index)
    for index in range(len(batches)):
        finish(index)

    for stage in stages:
        @pl.when(section == 0)
        def _():
            for off in range(1, tensors):
                entering(stage, off).wait_send()

        @pl.when(section > 0)
        def _():
            for at in range(chips):
                swap_half(stage, core, at).wait_send()

        @pl.when(section < sections - 1)
        def _():
            send_before(stage).wait_send()
            for at in range(chips):
                for target in range(chips):
                    send_sum(stage, target, at).wait_send()

        for at in range(chips):
            send_part(stage, at).wait_send()

            @pl.when(chip != at)
            def _():
                send_piece(stage, at).wait_send()


def emit_kernel(hidden_ref, keys_ref, values_ref, out_hidden, out_keys, out_values):
    out_hidden[...] = hidden_ref[...]
    out_keys[...] = keys_ref[...]
    out_values[...] = values_ref[...]


def solution(mesh):
    sections = mesh.shape["section"]
    tensors = mesh.shape["tensor"]
    chips = tensors // 2

    def per_device(
        inputs, gains, w_query, w_key, w_value, w_out, key_cache, value_cache, cache_lens, exit_plan
    ):
        rows, width = inputs.shape
        features = gains.shape[1]
        query_width = w_query.shape[2]
        kv_width = w_key.shape[2]
        heads = query_width // HEAD_DIM
        groups_per_kv = query_width // kv_width
        slot = -(-heads // 8) * 8
        slots = key_cache.shape[2]
        any_spec = pl.BlockSpec(memory_space=pl.ANY)
        vmem_spec = pl.BlockSpec(memory_space=pltpu.VMEM)
        bf16, f32 = jnp.bfloat16, jnp.float32
        batches = split_rows(rows)

        def stage_scratch(count):
            def blocks(*shape):
                return pltpu.VMEM((*shape, count, width), bf16)

            def sems(*shape):
                return pltpu.SemaphoreType.DMA(shape)

            return dict(
                hid=blocks(2, chips), before=blocks(chips), part=blocks(chips),
                part_in=blocks(chips), chip_sum=blocks(chips), sums_in=blocks(chips, chips),
                piece_in=blocks(chips), enter_send=sems(tensors), enter_recv=sems(2, chips),
                half_send=sems(chips), half_recv=sems(chips), before_send=sems(1),
                before_recv=sems(1), part_send=sems(chips), part_recv=sems(chips),
                sums_send=sems(chips, chips), sums_recv=sems(chips, chips),
                piece_send=sems(chips), piece_recv=sems(chips),
            )

        results = pl.pallas_call(
            functools.partial(relay_kernel, sections, tensors, groups_per_kv, batches),
            out_shape=(
                jax.ShapeDtypeStruct((1, rows, width), bf16),
                jax.ShapeDtypeStruct((1, rows, kv_width), bf16),
                jax.ShapeDtypeStruct((1, rows, kv_width), bf16),
            ),
            in_specs=[any_spec] * 10,
            out_specs=(vmem_spec,) * 3,
            scratch_shapes=[
                pltpu.VMEM((features, query_width), bf16),
                pltpu.VMEM((features, kv_width), bf16),
                pltpu.VMEM((features, kv_width), bf16),
                pltpu.VMEM((query_width, features), bf16),
                pltpu.VMEM((rows, slots, kv_width), bf16),
                pltpu.VMEM((rows, slots, kv_width), bf16),
                pltpu.VMEM((1, features), f32),
                pltpu.VMEM((rows, width), bf16),
                pltpu.VMEM((rows, features), bf16),
                pltpu.VMEM((rows, HEAD_DIM), f32),
                pltpu.VMEM((2, rows, HEAD_DIM), f32),
                pltpu.VMEM((rows * slot, slots), f32),
                pltpu.VMEM((rows * slot, HEAD_DIM), f32),
                pltpu.VMEM((rows * slot, slots), f32),
                pltpu.VMEM((rows * slot, HEAD_DIM), f32),
                pltpu.VMEM((rows * slot, HEAD_DIM), f32),
                pltpu.VMEM((rows * slot, HEAD_DIM), f32),
                pltpu.SMEM((rows,), jnp.int32),
                pltpu.SMEM((rows,), jnp.int32),
                pltpu.SemaphoreType.DMA((10,)),
                tuple(stage_scratch(count) for _, count in batches),
            ],
            compiler_params=pltpu.CompilerParams(
                collective_id=0, has_side_effects=True, vmem_limit_bytes=48 * 1024 * 1024
            ),
            name="relay",
        )(
            *(
                pltpu.with_memory_space_constraint(array, pltpu.HBM)
                for array in (
                    cache_lens, exit_plan, inputs, gains, w_query, w_key, w_value, w_out,
                    key_cache, value_cache,
                )
            )
        )
        return pl.pallas_call(
            emit_kernel,
            out_shape=tuple(jax.ShapeDtypeStruct(r.shape, r.dtype) for r in results),
            in_specs=[vmem_spec] * 3,
            out_specs=(vmem_spec,) * 3,
            compiler_params=pltpu.CompilerParams(vmem_limit_bytes=1024 * 1024),
            name="emit",
        )(*results)

    return jax.shard_map(
        per_device,
        mesh=mesh,
        in_specs=(
            P("group", "tensor"),
            P("section", None),
            P("section", None, "tensor"),
            P("section", None, "tensor"),
            P("section", None, "tensor"),
            P("section", "tensor", None),
            P("section", "group", None, "tensor"),
            P("section", "group", None, "tensor"),
            P("group"),
            P("group"),
        ),
        out_specs=(
            P("section", "group", "tensor"),
            P("section", "group", "tensor"),
            P("section", "group", "tensor"),
        ),
        check_vma=False,
    )
```

```python
import functools
import math

import jax
import jax.numpy as jnp
from jax import lax
from jax.experimental import pallas as pl
from jax.experimental.pallas import tpu as pltpu
from jax.sharding import PartitionSpec as P

HEAD_DIM = 128
NORM_EPSILON = 1e-05
ROPE_BASE = 500000.0
MASKED_SCORE = -1e30
MESH = pl.DeviceIdType.MESH


HALF_TILE = 4
TILE = 8
PADDED = 16


def row_of(batch, index):
    if index < TILE:
        return batch * TILE + index
    return 2 * TILE + HALF_TILE * batch + (index - TILE) % HALF_TILE


def relay_kernel(
    sections, tensors, groups_per_kv,
    lens_ref, plan_ref, inputs_ref, gains_ref, wq_ref, wk_ref, wv_ref, wo_ref, kc_ref, vc_ref,
    out_hidden, out_keys, out_values,
    wq, wk, wv, wo, kc, vc, gain, own, normed,
    pos, running, mask, queries, scores, score_new, values_new, attended,
    final, tail_keys, tail_values,
    lens, plan, load_sem, stages,
):
    width = own.shape[1]
    live = TILE + HALF_TILE
    batches = range(len(stages))
    chips = tensors // 2
    blocks = chips + chips // 2
    pieces = ((0, chips // 2), (chips // 2, blocks))
    kv_local = wk.shape[1] // HEAD_DIM
    heads = kv_local * groups_per_kv
    slot = queries.shape[0] // (PADDED * len(stages))
    slots = kc.shape[1]
    section = lax.axis_index("section")
    me = lax.axis_index("tensor")
    chip = me // 2
    core = lax.rem(me, 2)
    sibling = {"tensor": 2 * chip + 1 - core}
    inner = section < sections - 1
    last = section == sections - 1

    def load(source, target, index):
        return pltpu.make_async_copy(source, target, load_sem.at[index])

    def remote(source, target, send_sem, recv_sem, device):
        return pltpu.make_async_remote_copy(
            src_ref=source, dst_ref=target, send_sem=send_sem, recv_sem=recv_sem,
            device_id=device, device_id_type=MESH,
        )

    loads = dict(
        gain=load(gains_ref, gain, 0),
        wk=load(wk_ref.at[0], wk, 1),
        wv=load(wv_ref.at[0], wv, 2),
        wq=load(wq_ref.at[0], wq, 3),
        kc=load(kc_ref.at[0], kc, 4),
        vc=load(vc_ref.at[0], vc, 5),
        wo=load(wo_ref.at[0], wo, 6),
        lens=load(lens_ref, lens, 8),
        plan=load(plan_ref, plan, 9),
    )
    own_entering = load(inputs_ref, own, 7)

    @pl.when(section == 0)
    def _():
        own_entering.start()

    for name in ("lens", "plan", "gain", "wk", "wv", "wq", "kc"):
        loads[name].start()

    @pl.when(section > 0)
    def _():
        for name in ("vc", "wo"):
            loads[name].start()

    barrier = pltpu.get_barrier_semaphore()

    def greet(device):
        pl.semaphore_signal(barrier, inc=1, device_id=device, device_id_type=MESH)

    for off in range(1, tensors):
        greet({"tensor": lax.rem(me + off, tensors)})

    pl.semaphore_wait(barrier, (tensors - 1) + chips * (section > 0).astype(jnp.int32))

    @pl.when(section > 0)
    def _():
        for other in range(chips):
            greet({"section": section - 1, "tensor": 2 * other + core})

    @pl.when(inner)
    def _():
        for other in range(chips):
            greet({"section": section + 1, "tensor": 2 * other + core})

    def entering(stage, off):
        return remote(
            stage["enter"].at[core, chip], stage["enter"].at[core, chip],
            stage["enter_send"].at[off], stage["enter_recv"].at[core, chip],
            {"tensor": lax.rem(me + off, tensors)},
        )

    def span_of(piece):
        first, end = pieces[piece]
        return pl.ds(first, end - first)

    def swap_half(stage, parity, piece):
        part_of = stage["hid"].at[parity, span_of(piece)]
        return remote(
            part_of, part_of, stage["half_send"].at[piece], stage["half_recv"].at[piece], sibling
        )

    def send_sum(stage, target, piece):
        return remote(
            stage["chip_sum"].at[span_of(piece)], stage["sums_in"].at[chip, span_of(piece)],
            stage["sums_send"].at[target, piece], stage["sums_recv"].at[chip, piece],
            {"section": section + 1, "tensor": 2 * target + core},
        )

    def send_before(stage):
        return remote(
            stage["hid"].at[core], stage["before"], stage["before_send"].at[0],
            stage["before_recv"].at[0], {"section": section + 1},
        )

    def send_part(stage, piece):
        return remote(
            stage["part"].at[span_of(piece)], stage["part_in"].at[span_of(piece)],
            stage["part_send"].at[piece], stage["part_recv"].at[piece], sibling,
        )

    def send_owned(stage, at, which):
        block = at if which == 0 else chips + at // 2
        return remote(
            stage["chip_sum"].at[block], stage["owned_in"].at[chip, which],
            stage["owned_send"].at[at, which], stage["owned_recv"].at[chip, which],
            {"tensor": 2 * at + core},
        )

    closing = []
    for step in range(1, chips):
        other = lax.rem(chip + step, chips)
        closing += [2 * other + core, 2 * other + 1 - core]
    closing += [2 * chip + 1 - core, me]

    def send_direct(stage, order):
        return remote(
            stage["direct"].at[order], stage["direct_in"].at[me],
            stage["direct_send"].at[order], stage["direct_recv"].at[me],
            {"tensor": closing[order]},
        )

    @pl.when(section == 0)
    def _():
        own_entering.wait()
        stages[0]["enter"][core, chip, :TILE, :] = own[:TILE, :]
        stages[0]["enter"][core, chip, TILE:, :] = own[2 * TILE :, :]
        stages[1]["enter"][core, chip] = own[TILE : 2 * TILE, :]
        for stage in stages:
            for off in range(1, tensors):
                entering(stage, off).start()
        for name in ("vc", "wo"):
            loads[name].start()

    for name in ("lens", "plan"):
        loads[name].wait()
    lane = lax.broadcasted_iota(jnp.int32, (slot, slots), 1)
    for batch in batches:
        for index in range(PADDED):
            row = row_of(batch, index)
            length = lens[row]
            place = slice(index, index + 1)
            pos[batch, place, :] = jnp.full((1, HEAD_DIM), length, jnp.int32).astype(jnp.float32)
            planned = jnp.full((1, HEAD_DIM), plan[row], jnp.int32)
            running[0, batch, place, :] = (planned > section).astype(jnp.float32)
            running[1, batch, place, :] = (planned > section - 1).astype(jnp.float32)
            if index < live:
                line = (batch * PADDED + index) * slot
                mask[line : line + slot, :] = (lane < length).astype(jnp.float32)
    half_lane = lax.broadcasted_iota(jnp.int32, (PADDED, HEAD_DIM), 1)
    half = HEAD_DIM // 2
    step_at = jnp.where(half_lane < half, half_lane, half_lane - half).astype(jnp.float32)
    frequency = jnp.exp(step_at * (-2.0 * math.log(ROPE_BASE) / HEAD_DIM))
    turns = []
    for batch in batches:
        angles = pos[batch] * frequency
        sin_part = jnp.sin(angles)
        turns.append((jnp.cos(angles), jnp.where(half_lane < half, -sin_part, sin_part)))
    attended[...] = jnp.zeros_like(attended)
    if heads < slot:
        queries[...] = jnp.zeros_like(queries)
        score_new[...] = jnp.zeros_like(score_new)
        values_new[...] = jnp.zeros_like(values_new)

    upper = lax.broadcasted_iota(jnp.int32, (TILE, width), 0) < HALF_TILE

    def turn(block):
        return pltpu.roll(block, HALF_TILE, 0)

    def pack(first, second):
        return jnp.where(upper[:, : first.shape[1]], first, turn(second))

    def receive(batch):
        stage = stages[batch]
        hid = stage["hid"]

        @pl.when(section == 0)
        def _():
            enter, shared = stage["enter"], stages[0]["enter"]
            for off in range(1, tensors):
                other = lax.rem(me + off, tensors)
                at = (lax.rem(other, 2), other // 2)
                remote(
                    enter.at[at], enter.at[at], stage["enter_send"].at[off],
                    stage["enter_recv"].at[at], sibling,
                ).wait_recv()
            for parity in range(2):
                for at in range(chips):
                    hid[parity, at] = enter[parity, at, :TILE, :]
                for pair in range(chips // 2):
                    tails = [
                        shared[parity, 2 * pair + side, TILE:, :].astype(jnp.float32)
                        for side in range(2)
                    ]
                    if batch == 0:
                        packed = jnp.where(upper, tails[0], turn(tails[1]))
                    else:
                        packed = jnp.where(upper, turn(tails[0]), tails[1])
                    hid[parity, chips + pair] = packed.astype(jnp.bfloat16)

        @pl.when(section > 0)
        def _():
            before, sums_in = stage["before"], stage["sums_in"]
            remote(
                before, before, stage["before_send"].at[0], stage["before_recv"].at[0],
                {"section": section - 1},
            ).wait_recv()
            for piece, (first, end) in enumerate(pieces):
                for source in range(chips):
                    arrived = sums_in.at[source, span_of(piece)]
                    remote(
                        arrived, arrived, stage["sums_send"].at[source, piece],
                        stage["sums_recv"].at[source, piece], {"section": section - 1},
                    ).wait_recv()
                for block in range(first, end):
                    total = jnp.zeros((TILE, width), jnp.float32)
                    for source in range(chips):
                        total = total + sums_in[source, block].astype(jnp.float32)
                    wide = before[block].astype(jnp.float32)
                    rows_on = slice(0, TILE) if block < chips else slice(TILE, PADDED)
                    on = running[1, batch, rows_on, :1]
                    hid[core, block] = (wide + on * total).astype(jnp.bfloat16)
                swap_half(stage, core, piece).start()
            for piece in range(len(pieces)):
                swap_half(stage, 1 - core, piece).wait_recv()

        if batch > 0:
            @pl.when(inner)
            def _():
                send_before(stage).start()

    inv_root = 1.0 / math.sqrt(HEAD_DIM)
    head_of = lax.broadcasted_iota(jnp.int32, (slot, HEAD_DIM), 0) // groups_per_kv

    def compute(batch):
        stage = stages[batch]
        hid = stage["hid"]
        cos_here, sin_here = turns[batch]
        first_line = batch * PADDED * slot

        def rotate(vectors):
            return vectors * cos_here + pltpu.roll(vectors, half, 1) * sin_here

        if batch == 0:
            for name in ("gain", "wk", "wv", "wq", "kc", "vc"):
                loads[name].wait()

        squares = jnp.zeros((TILE, 1), jnp.float32)
        tail_squares = jnp.zeros((TILE, 1), jnp.float32)
        for parity in range(2):
            for block in range(blocks):
                wide = hid[parity, block].astype(jnp.float32)
                square = jnp.sum(wide * wide, axis=-1, keepdims=True)
                if block < chips:
                    squares = squares + square
                else:
                    tail_squares = tail_squares + square
        tail_squares = jnp.broadcast_to(tail_squares, (TILE, HEAD_DIM))
        tail_squares = (tail_squares + turn(tail_squares))[:, :1]
        scale = lax.rsqrt(squares / (tensors * width) + NORM_EPSILON)
        tail_scale = lax.rsqrt(tail_squares / (tensors * width) + NORM_EPSILON)
        for parity in range(2):
            for pair in range(chips // 2):
                columns = [
                    slice((2 * at + parity) * width, (2 * at + parity + 1) * width)
                    for at in (2 * pair, 2 * pair + 1)
                ]
                gains = [jnp.broadcast_to(gain[:, at], (TILE, width)) for at in columns]
                tail = hid[parity, chips + pair].astype(jnp.float32)
                tail = tail * tail_scale * jnp.where(upper, gains[0], gains[1])
                for side, at in enumerate(columns):
                    wide = hid[parity, 2 * pair + side].astype(jnp.float32)
                    wide = wide * scale * gains[side]
                    both = jnp.concatenate([wide, tail if side == 0 else turn(tail)], axis=0)
                    normed[:, at] = both.astype(jnp.bfloat16)

        entered = normed[...]
        key_new = jnp.dot(entered, wk[...], preferred_element_type=jnp.float32)
        value_new = jnp.dot(entered, wv[...], preferred_element_type=jnp.float32)
        tail_values[batch] = value_new[TILE:, :]
        value_new = value_new.astype(jnp.bfloat16)
        main_rows = slice(batch * TILE, (batch + 1) * TILE)
        out_values[0, main_rows, :] = value_new[:TILE, :]
        keys = []
        values = []
        for kv in range(kv_local):
            at = slice(kv * HEAD_DIM, (kv + 1) * HEAD_DIM)
            rotated = rotate(key_new[:, at])
            tail_keys[batch, :, at] = rotated[TILE:, :]
            rotated = rotated.astype(jnp.bfloat16)
            out_keys[0, main_rows, at] = rotated[:TILE, :]
            keys.append(rotated.astype(jnp.float32))
            values.append(value_new[:, at].astype(jnp.float32))

        tile = min(256, heads * HEAD_DIM)
        for start in range(0, heads * HEAD_DIM, tile):
            product = jnp.dot(
                entered, wq[:, start : start + tile], preferred_element_type=jnp.float32
            )
            for side in range(tile // HEAD_DIM):
                head = start // HEAD_DIM + side
                kv = head // groups_per_kv
                query = rotate(product[:, side * HEAD_DIM : (side + 1) * HEAD_DIM])
                query = query.astype(jnp.bfloat16).astype(jnp.float32)
                at = pl.ds(first_line + head, PADDED, stride=slot)
                queries[at, :] = query
                score = jnp.sum(query * keys[kv], axis=-1, keepdims=True) * inv_root
                score_new[at, :] = jnp.broadcast_to(score, (PADDED, HEAD_DIM))
                values_new[at, :] = values[kv]

        for index in range(live):
            at = slice(first_line + index * slot, first_line + (index + 1) * slot)
            query = queries[at, :]
            spread = jnp.concatenate(
                [jnp.where(head_of == kv, query, 0.0) for kv in range(kv_local)], axis=1
            ).astype(jnp.bfloat16)
            scores[at, :] = lax.dot_general(
                spread, kc[row_of(batch, index)], (((1,), (1,)), ((), ())),
                preferred_element_type=jnp.float32,
            )

        lines = slice(first_line, first_line + live * slot)
        old = jnp.where(mask[lines, :] > 0.0, scores[lines, :] * inv_root, MASKED_SCORE)
        new = score_new[lines, :1]
        highest = jnp.maximum(jnp.max(old, axis=-1, keepdims=True), new)
        weight_old = jnp.exp(old - highest)
        weight_new = jnp.exp(new - highest)
        denominator = jnp.sum(weight_old, axis=-1, keepdims=True) + weight_new
        scores[lines, :] = weight_old / denominator
        weight_new = (weight_new / denominator).astype(jnp.bfloat16).astype(jnp.float32)
        values_new[lines, :] = values_new[lines, :] * weight_new

        for index in range(live):
            at = slice(first_line + index * slot, first_line + (index + 1) * slot)
            mixed = jnp.dot(
                scores[at, :].astype(jnp.bfloat16), vc[row_of(batch, index)],
                preferred_element_type=jnp.float32,
            )
            taken = mixed[:, :HEAD_DIM]
            for kv in range(1, kv_local):
                taken = jnp.where(
                    head_of == kv, mixed[:, kv * HEAD_DIM : (kv + 1) * HEAD_DIM], taken
                )
            attended[at, :] = taken + values_new[at, :]

        flat = jnp.concatenate(
            [
                attended[pl.ds(first_line + head, PADDED, stride=slot), :].astype(jnp.bfloat16)
                for head in range(heads)
            ],
            axis=1,
        )

        if batch == 0:
            loads["wo"].wait()

            @pl.when(inner)
            def _():
                pl.semaphore_wait(barrier, chips)
                send_before(stage).start()

        def project(order):
            parity, at = (1 - core, order) if order < chips else (core, order - chips)
            start = jnp.where(last, closing[order], 2 * at + parity) * width
            columns = pl.ds(pl.multiple_of(start, width), width)
            return jnp.dot(flat, wo[:, columns], preferred_element_type=jnp.float32)

        part, part_in, chip_sum = stage["part"], stage["part_in"], stage["chip_sum"]
        direct = stage["direct"]
        tail = None
        for order in range(chips):
            product = project(order)
            direct[order] = product.astype(jnp.bfloat16)
            part[order] = product[:TILE, :].astype(jnp.bfloat16)
            if order % 2 == 0:
                tail = product[TILE:, :]
            else:
                part[chips + order // 2] = pack(tail, product[TILE:, :]).astype(jnp.bfloat16)

            @pl.when(last)
            def _():
                send_direct(stage, order).start()

            if order + 1 in (chips // 2, chips):
                @pl.when(inner)
                def _():
                    send_part(stage, 0 if order + 1 < chips else 1).start()

        mine = [project(order) for order in range(chips, tensors)]

        @pl.when(last)
        def _():
            for order in range(chips, tensors - 1):
                direct[order] = mine[order - chips].astype(jnp.bfloat16)
                send_direct(stage, order).start()
            final[batch] = mine[-1]

        @pl.when(inner)
        def _():
            for piece, (first, end) in enumerate(pieces):
                send_part(stage, piece).wait_recv()
                for block in range(first, end):
                    if block < chips:
                        own_sum = mine[block][:TILE, :]
                    else:
                        pair = 2 * (block - chips)
                        own_sum = pack(mine[pair][TILE:, :], mine[pair + 1][TILE:, :])
                    chip_sum[block] = (
                        own_sum + part_in[block].astype(jnp.float32)
                    ).astype(jnp.bfloat16)
                for target in range(chips):
                    send_sum(stage, target, piece).start()
            for at in range(chips):
                @pl.when(chip != at)
                def _():
                    for which in range(2):
                        send_owned(stage, at, which).start()

    odd = lax.rem(chip, 2) == 1

    def finish(batch):
        stage = stages[batch]

        @pl.when(last)
        def _():
            total = final[batch]
            for off in range(1, tensors):
                other = lax.rem(me + off, tensors)
                arrived = stage["direct_in"].at[other]
                remote(
                    arrived, arrived, stage["direct_send"].at[off - 1],
                    stage["direct_recv"].at[other], sibling,
                ).wait_recv()
                total = total + arrived[...].astype(jnp.float32)
            final[batch] = total

        @pl.when(inner)
        def _():
            owned_in, chip_sum = stage["owned_in"], stage["chip_sum"]
            owned_in[chip, 0] = chip_sum[chip]
            owned_in[chip, 1] = chip_sum[chips + chip // 2]
            totals = [jnp.zeros((TILE, width), jnp.float32) for _ in range(2)]
            for source in range(chips):
                @pl.when(chip != source)
                def _():
                    for which in range(2):
                        arrived = owned_in.at[source, which]
                        remote(
                            arrived, arrived, stage["owned_send"].at[source, which],
                            stage["owned_recv"].at[source, which], sibling,
                        ).wait_recv()

                for which in range(2):
                    totals[which] = totals[which] + owned_in[source, which].astype(jnp.float32)
            final[batch, :TILE, :] = totals[0]
            final[batch, TILE:, :] = jnp.where(odd, turn(totals[1]), totals[1])

        hid = stage["hid"]
        wide = hid[core, chip].astype(jnp.float32)
        main_on = running[0, batch, :TILE, :1]
        main = wide + main_on * final[batch, :TILE, :]
        out_hidden[0, batch * TILE : (batch + 1) * TILE, :] = main.astype(jnp.bfloat16)
        wide = hid[core, chips + chip // 2].astype(jnp.float32)
        wide = jnp.where(odd, turn(wide), wide)
        return wide + running[0, batch, TILE:, :1] * final[batch, TILE:, :]

    for batch in batches:
        receive(batch)
        compute(batch)
    tails = slice(2 * TILE, 3 * TILE)
    for target, held in ((out_keys, tail_keys), (out_values, tail_values)):
        columns = held.shape[2]
        for start in range(0, columns, min(columns, width)):
            at = slice(start, start + min(columns, width))
            packed = pack(held[0, :, at], held[1, :, at])
            target[0, tails, at] = packed.astype(jnp.bfloat16)
    out_hidden[0, tails, :] = pack(finish(0), finish(1)).astype(jnp.bfloat16)

    for stage in stages:
        @pl.when(section == 0)
        def _():
            for off in range(1, tensors):
                entering(stage, off).wait_send()

        @pl.when(section > 0)
        def _():
            for piece in range(len(pieces)):
                swap_half(stage, core, piece).wait_send()

        @pl.when(last)
        def _():
            for order in range(tensors - 1):
                send_direct(stage, order).wait_send()

        @pl.when(inner)
        def _():
            send_before(stage).wait_send()
            for piece in range(len(pieces)):
                send_part(stage, piece).wait_send()
                for target in range(chips):
                    send_sum(stage, target, piece).wait_send()
            for at in range(chips):
                @pl.when(chip != at)
                def _():
                    for which in range(2):
                        send_owned(stage, at, which).wait_send()


def emit_kernel(hidden_ref, keys_ref, values_ref, out_hidden, out_keys, out_values):
    out_hidden[...] = hidden_ref[...]
    out_keys[...] = keys_ref[...]
    out_values[...] = values_ref[...]


def solution(mesh):
    sections = mesh.shape["section"]
    tensors = mesh.shape["tensor"]
    chips = tensors // 2

    def per_device(
        inputs, gains, w_query, w_key, w_value, w_out, key_cache, value_cache, cache_lens, exit_plan
    ):
        rows, width = inputs.shape
        features = gains.shape[1]
        query_width = w_query.shape[2]
        kv_width = w_key.shape[2]
        heads = query_width // HEAD_DIM
        groups_per_kv = query_width // kv_width
        slot = -(-heads // 8) * 8
        slots = key_cache.shape[2]
        any_spec = pl.BlockSpec(memory_space=pl.ANY)
        vmem_spec = pl.BlockSpec(memory_space=pltpu.VMEM)
        bf16, f32 = jnp.bfloat16, jnp.float32
        batches = 2
        lines = batches * PADDED * slot
        blocks = chips + chips // 2

        def stage_scratch(batch):
            def vmem(*shape):
                return pltpu.VMEM((*shape, width), bf16)

            def sems(*shape):
                return pltpu.SemaphoreType.DMA(shape)

            return dict(
                enter=vmem(2, chips, PADDED if batch == 0 else TILE),
                hid=vmem(2, blocks, TILE), before=vmem(blocks, TILE), part=vmem(blocks, TILE),
                part_in=vmem(blocks, TILE), chip_sum=vmem(blocks, TILE),
                sums_in=vmem(chips, blocks, TILE), owned_in=vmem(chips, 2, TILE),
                direct=vmem(tensors - 1, PADDED), direct_in=vmem(tensors, PADDED),
                enter_send=sems(tensors), enter_recv=sems(2, chips),
                half_send=sems(2), half_recv=sems(2), before_send=sems(1),
                before_recv=sems(1), part_send=sems(2), part_recv=sems(2),
                sums_send=sems(chips, 2), sums_recv=sems(chips, 2),
                owned_send=sems(chips, 2), owned_recv=sems(chips, 2),
                direct_send=sems(tensors - 1), direct_recv=sems(tensors),
            )

        results = pl.pallas_call(
            functools.partial(relay_kernel, sections, tensors, groups_per_kv),
            out_shape=(
                jax.ShapeDtypeStruct((1, rows, width), bf16),
                jax.ShapeDtypeStruct((1, rows, kv_width), bf16),
                jax.ShapeDtypeStruct((1, rows, kv_width), bf16),
            ),
            in_specs=[any_spec] * 10,
            out_specs=(vmem_spec,) * 3,
            scratch_shapes=[
                pltpu.VMEM((features, query_width), bf16),
                pltpu.VMEM((features, kv_width), bf16),
                pltpu.VMEM((features, kv_width), bf16),
                pltpu.VMEM((query_width, features), bf16),
                pltpu.VMEM((rows, slots, kv_width), bf16),
                pltpu.VMEM((rows, slots, kv_width), bf16),
                pltpu.VMEM((1, features), f32),
                pltpu.VMEM((rows, width), bf16),
                pltpu.VMEM((PADDED, features), bf16),
                pltpu.VMEM((batches, PADDED, HEAD_DIM), f32),
                pltpu.VMEM((2, batches, PADDED, HEAD_DIM), f32),
                pltpu.VMEM((lines, slots), f32),
                pltpu.VMEM((lines, HEAD_DIM), f32),
                pltpu.VMEM((lines, slots), f32),
                pltpu.VMEM((lines, HEAD_DIM), f32),
                pltpu.VMEM((lines, HEAD_DIM), f32),
                pltpu.VMEM((lines, HEAD_DIM), f32),
                pltpu.VMEM((batches, PADDED, width), f32),
                pltpu.VMEM((batches, TILE, kv_width), f32),
                pltpu.VMEM((batches, TILE, kv_width), f32),
                pltpu.SMEM((rows,), jnp.int32),
                pltpu.SMEM((rows,), jnp.int32),
                pltpu.SemaphoreType.DMA((10,)),
                tuple(stage_scratch(batch) for batch in range(batches)),
            ],
            compiler_params=pltpu.CompilerParams(
                collective_id=0, has_side_effects=True, vmem_limit_bytes=48 * 1024 * 1024
            ),
            name="relay",
        )(
            *(
                pltpu.with_memory_space_constraint(array, pltpu.HBM)
                for array in (
                    cache_lens, exit_plan, inputs, gains, w_query, w_key, w_value, w_out,
                    key_cache, value_cache,
                )
            )
        )
        return pl.pallas_call(
            emit_kernel,
            out_shape=tuple(jax.ShapeDtypeStruct(r.shape, r.dtype) for r in results),
            in_specs=[vmem_spec] * 3,
            out_specs=(vmem_spec,) * 3,
            compiler_params=pltpu.CompilerParams(vmem_limit_bytes=1024 * 1024),
            name="emit",
        )(*results)

    return jax.shard_map(
        per_device,
        mesh=mesh,
        in_specs=(
            P("group", "tensor"),
            P("section", None),
            P("section", None, "tensor"),
            P("section", None, "tensor"),
            P("section", None, "tensor"),
            P("section", "tensor", None),
            P("section", "group", None, "tensor"),
            P("section", "group", None, "tensor"),
            P("group"),
            P("group"),
        ),
        out_specs=(
            P("section", "group", "tensor"),
            P("section", "group", "tensor"),
            P("section", "group", "tensor"),
        ),
        check_vma=False,
    )
```

```python
import functools
import math

import jax
import jax.numpy as jnp
from jax import lax
from jax.experimental import pallas as pl
from jax.experimental.pallas import tpu as pltpu
from jax.sharding import PartitionSpec as P

HEAD_DIM = 128
NORM_EPSILON = 1e-05
ROPE_BASE = 500000.0
MASKED_SCORE = -1e30
MESH = pl.DeviceIdType.MESH


HALF_TILE = 4
TILE = 8
PADDED = 16


def row_of(batch, index):
    if index < TILE:
        return batch * TILE + index
    return 2 * TILE + HALF_TILE * batch + (index - TILE) % HALF_TILE


def relay_kernel(
    sections, tensors, groups_per_kv,
    lens_ref, plan_ref, inputs_ref, gains_ref, wq_ref, wk_ref, wv_ref, wo_ref, kc_ref, vc_ref,
    out_hidden, out_keys, out_values,
    wq, wk, wv, wo, kc, vc, gain, own, normed,
    pos, running, mask, queries, scores, score_new, values_new, attended,
    final, tail_keys, tail_values,
    lens, plan, load_sem, stages,
):
    width = own.shape[1]
    live = TILE + HALF_TILE
    batches = range(len(stages))
    chips = tensors // 2
    blocks = chips + chips // 2
    pieces = ((0, chips // 2), (chips // 2, blocks))
    kv_local = wk.shape[1] // HEAD_DIM
    heads = kv_local * groups_per_kv
    slot = queries.shape[0] // (PADDED * len(stages))
    slots = kc.shape[1]
    section = lax.axis_index("section")
    me = lax.axis_index("tensor")
    chip = me // 2
    core = lax.rem(me, 2)
    sibling = {"tensor": 2 * chip + 1 - core}
    inner = section < sections - 1
    last = section == sections - 1

    def load(source, target, index):
        return pltpu.make_async_copy(source, target, load_sem.at[index])

    def remote(source, target, send_sem, recv_sem, device):
        return pltpu.make_async_remote_copy(
            src_ref=source, dst_ref=target, send_sem=send_sem, recv_sem=recv_sem,
            device_id=device, device_id_type=MESH,
        )

    loads = dict(
        gain=load(gains_ref, gain, 0),
        wk=load(wk_ref.at[0], wk, 1),
        wv=load(wv_ref.at[0], wv, 2),
        wq=load(wq_ref.at[0], wq, 3),
        kc=load(kc_ref.at[0], kc, 4),
        vc=load(vc_ref.at[0], vc, 5),
        wo=load(wo_ref.at[0], wo, 6),
        lens=load(lens_ref, lens, 8),
        plan=load(plan_ref, plan, 9),
    )
    own_entering = load(inputs_ref, own, 7)

    @pl.when(section == 0)
    def _():
        own_entering.start()

    for name in ("lens", "plan", "gain", "wk", "wv", "wq", "kc", "vc", "wo"):
        loads[name].start()

    barrier = pltpu.get_barrier_semaphore()

    def greet(device):
        pl.semaphore_signal(barrier, inc=1, device_id=device, device_id_type=MESH)

    for off in range(1, tensors):
        greet({"tensor": lax.rem(me + off, tensors)})

    pl.semaphore_wait(barrier, (tensors - 1) + chips * (section > 0).astype(jnp.int32))

    @pl.when(section > 0)
    def _():
        for other in range(chips):
            greet({"section": section - 1, "tensor": 2 * other + core})

    @pl.when(inner)
    def _():
        for other in range(chips):
            greet({"section": section + 1, "tensor": 2 * other + core})

    def entering(stage, off):
        return remote(
            stage["enter"].at[core, chip], stage["enter"].at[core, chip],
            stage["enter_send"].at[off], stage["enter_recv"].at[core, chip],
            {"tensor": lax.rem(me + off, tensors)},
        )

    def span_of(piece):
        first, end = pieces[piece]
        return pl.ds(first, end - first)

    def swap_half(stage, parity, piece):
        part_of = stage["hid"].at[parity, span_of(piece)]
        return remote(
            part_of, part_of, stage["half_send"].at[piece], stage["half_recv"].at[piece], sibling
        )

    def send_sum(stage, target, piece):
        return remote(
            stage["chip_sum"].at[span_of(piece)], stage["sums_in"].at[chip, span_of(piece)],
            stage["sums_send"].at[target, piece], stage["sums_recv"].at[chip, piece],
            {"section": section + 1, "tensor": 2 * target + core},
        )

    def send_before(stage):
        return remote(
            stage["hid"].at[core], stage["before"], stage["before_send"].at[0],
            stage["before_recv"].at[0], {"section": section + 1},
        )

    def send_part(stage, piece):
        return remote(
            stage["part"].at[span_of(piece)], stage["part_in"].at[span_of(piece)],
            stage["part_send"].at[piece], stage["part_recv"].at[piece], sibling,
        )

    def send_owned(stage, at, which):
        block = at if which == 0 else chips + at // 2
        return remote(
            stage["chip_sum"].at[block], stage["owned_in"].at[chip, which],
            stage["owned_send"].at[at, which], stage["owned_recv"].at[chip, which],
            {"tensor": 2 * at + core},
        )

    closing = []
    for step in range(1, chips):
        other = lax.rem(chip + step, chips)
        closing += [2 * other + core, 2 * other + 1 - core]
    closing += [2 * chip + 1 - core, me]

    def send_direct(stage, order):
        return remote(
            stage["direct"].at[order], stage["direct_in"].at[me],
            stage["direct_send"].at[order], stage["direct_recv"].at[me],
            {"tensor": closing[order]},
        )

    @pl.when(section == 0)
    def _():
        own_entering.wait()
        stages[0]["enter"][core, chip, :TILE, :] = own[:TILE, :]
        stages[0]["enter"][core, chip, TILE:, :] = own[2 * TILE :, :]
        stages[1]["enter"][core, chip] = own[TILE : 2 * TILE, :]
        for stage in stages:
            for off in range(1, tensors):
                entering(stage, off).start()

    for name in ("lens", "plan"):
        loads[name].wait()
    lane = lax.broadcasted_iota(jnp.int32, (slot, slots), 1)
    for batch in batches:
        for index in range(PADDED):
            row = row_of(batch, index)
            length = lens[row]
            place = slice(index, index + 1)
            pos[batch, place, :] = jnp.full((1, HEAD_DIM), length, jnp.int32).astype(jnp.float32)
            planned = jnp.full((1, HEAD_DIM), plan[row], jnp.int32)
            running[0, batch, place, :] = (planned > section).astype(jnp.float32)
            running[1, batch, place, :] = (planned > section - 1).astype(jnp.float32)
            if index < live:
                line = (batch * PADDED + index) * slot
                mask[line : line + slot, :] = (lane < length).astype(jnp.float32)
    half_lane = lax.broadcasted_iota(jnp.int32, (PADDED, HEAD_DIM), 1)
    half = HEAD_DIM // 2
    step_at = jnp.where(half_lane < half, half_lane, half_lane - half).astype(jnp.float32)
    frequency = jnp.exp(step_at * (-2.0 * math.log(ROPE_BASE) / HEAD_DIM))
    turns = []
    for batch in batches:
        angles = pos[batch] * frequency
        sin_part = jnp.sin(angles)
        turns.append((jnp.cos(angles), jnp.where(half_lane < half, -sin_part, sin_part)))
    attended[...] = jnp.zeros_like(attended)
    if heads < slot:
        queries[...] = jnp.zeros_like(queries)
        score_new[...] = jnp.zeros_like(score_new)
        values_new[...] = jnp.zeros_like(values_new)

    upper = lax.broadcasted_iota(jnp.int32, (TILE, width), 0) < HALF_TILE

    def turn(block):
        return pltpu.roll(block, HALF_TILE, 0)

    def pack(first, second):
        return jnp.where(upper[:, : first.shape[1]], first, turn(second))

    def receive(batch):
        stage = stages[batch]
        hid = stage["hid"]

        @pl.when(section == 0)
        def _():
            enter, shared = stage["enter"], stages[0]["enter"]
            for off in range(1, tensors):
                other = lax.rem(me + off, tensors)
                at = (lax.rem(other, 2), other // 2)
                remote(
                    enter.at[at], enter.at[at], stage["enter_send"].at[off],
                    stage["enter_recv"].at[at], sibling,
                ).wait_recv()
            for parity in range(2):
                for at in range(chips):
                    hid[parity, at] = enter[parity, at, :TILE, :]
                for pair in range(chips // 2):
                    tails = [
                        shared[parity, 2 * pair + side, TILE:, :].astype(jnp.float32)
                        for side in range(2)
                    ]
                    if batch == 0:
                        packed = jnp.where(upper, tails[0], turn(tails[1]))
                    else:
                        packed = jnp.where(upper, turn(tails[0]), tails[1])
                    hid[parity, chips + pair] = packed.astype(jnp.bfloat16)

        @pl.when(section > 0)
        def _():
            before, sums_in = stage["before"], stage["sums_in"]
            remote(
                before, before, stage["before_send"].at[0], stage["before_recv"].at[0],
                {"section": section - 1},
            ).wait_recv()
            for piece, (first, end) in enumerate(pieces):
                for source in range(chips):
                    arrived = sums_in.at[source, span_of(piece)]
                    remote(
                        arrived, arrived, stage["sums_send"].at[source, piece],
                        stage["sums_recv"].at[source, piece], {"section": section - 1},
                    ).wait_recv()
                for block in range(first, end):
                    total = jnp.zeros((TILE, width), jnp.float32)
                    for source in range(chips):
                        total = total + sums_in[source, block].astype(jnp.float32)
                    wide = before[block].astype(jnp.float32)
                    rows_on = slice(0, TILE) if block < chips else slice(TILE, PADDED)
                    on = running[1, batch, rows_on, :1]
                    hid[core, block] = (wide + on * total).astype(jnp.bfloat16)
                swap_half(stage, core, piece).start()
            for piece in range(len(pieces)):
                swap_half(stage, 1 - core, piece).wait_recv()

    inv_root = 1.0 / math.sqrt(HEAD_DIM)
    head_of = lax.broadcasted_iota(jnp.int32, (slot, HEAD_DIM), 0) // groups_per_kv

    def compute(batch):
        stage = stages[batch]
        hid = stage["hid"]
        cos_here, sin_here = turns[batch]
        first_line = batch * PADDED * slot

        def rotate(vectors):
            return vectors * cos_here + pltpu.roll(vectors, half, 1) * sin_here

        if batch == 0:
            for name in ("gain", "wk", "wv", "wq", "kc", "vc"):
                loads[name].wait()

        squares = jnp.zeros((TILE, 1), jnp.float32)
        tail_squares = jnp.zeros((TILE, 1), jnp.float32)
        for parity in range(2):
            for block in range(blocks):
                wide = hid[parity, block].astype(jnp.float32)
                square = jnp.sum(wide * wide, axis=-1, keepdims=True)
                if block < chips:
                    squares = squares + square
                else:
                    tail_squares = tail_squares + square
        tail_squares = jnp.broadcast_to(tail_squares, (TILE, HEAD_DIM))
        tail_squares = (tail_squares + turn(tail_squares))[:, :1]
        scale = lax.rsqrt(squares / (tensors * width) + NORM_EPSILON)
        tail_scale = lax.rsqrt(tail_squares / (tensors * width) + NORM_EPSILON)
        for parity in range(2):
            for pair in range(chips // 2):
                columns = [
                    slice((2 * at + parity) * width, (2 * at + parity + 1) * width)
                    for at in (2 * pair, 2 * pair + 1)
                ]
                gains = [jnp.broadcast_to(gain[:, at], (TILE, width)) for at in columns]
                tail = hid[parity, chips + pair].astype(jnp.float32)
                tail = tail * tail_scale * jnp.where(upper, gains[0], gains[1])
                for side, at in enumerate(columns):
                    wide = hid[parity, 2 * pair + side].astype(jnp.float32)
                    wide = wide * scale * gains[side]
                    both = jnp.concatenate([wide, tail if side == 0 else turn(tail)], axis=0)
                    normed[:, at] = both.astype(jnp.bfloat16)

        entered = normed[...]
        key_new = jnp.dot(entered, wk[...], preferred_element_type=jnp.float32)
        value_new = jnp.dot(entered, wv[...], preferred_element_type=jnp.float32)
        tail_values[batch] = value_new[TILE:, :]
        value_new = value_new.astype(jnp.bfloat16)
        main_rows = slice(batch * TILE, (batch + 1) * TILE)
        out_values[0, main_rows, :] = value_new[:TILE, :]
        keys = []
        values = []
        for kv in range(kv_local):
            at = slice(kv * HEAD_DIM, (kv + 1) * HEAD_DIM)
            rotated = rotate(key_new[:, at])
            tail_keys[batch, :, at] = rotated[TILE:, :]
            rotated = rotated.astype(jnp.bfloat16)
            out_keys[0, main_rows, at] = rotated[:TILE, :]
            keys.append(rotated.astype(jnp.float32))
            values.append(value_new[:, at].astype(jnp.float32))

        tile = min(256, heads * HEAD_DIM)
        for start in range(0, heads * HEAD_DIM, tile):
            product = jnp.dot(
                entered, wq[:, start : start + tile], preferred_element_type=jnp.float32
            )
            for side in range(tile // HEAD_DIM):
                head = start // HEAD_DIM + side
                kv = head // groups_per_kv
                query = rotate(product[:, side * HEAD_DIM : (side + 1) * HEAD_DIM])
                query = query.astype(jnp.bfloat16).astype(jnp.float32)
                at = pl.ds(first_line + head, PADDED, stride=slot)
                queries[at, :] = query
                score = jnp.sum(query * keys[kv], axis=-1, keepdims=True) * inv_root
                score_new[at, :] = jnp.broadcast_to(score, (PADDED, HEAD_DIM))
                values_new[at, :] = values[kv]

        for index in range(live):
            at = slice(first_line + index * slot, first_line + (index + 1) * slot)
            query = queries[at, :]
            spread = jnp.concatenate(
                [jnp.where(head_of == kv, query, 0.0) for kv in range(kv_local)], axis=1
            ).astype(jnp.bfloat16)
            scores[at, :] = lax.dot_general(
                spread, kc[row_of(batch, index)], (((1,), (1,)), ((), ())),
                preferred_element_type=jnp.float32,
            )

        lines = slice(first_line, first_line + live * slot)
        old = jnp.where(mask[lines, :] > 0.0, scores[lines, :] * inv_root, MASKED_SCORE)
        new = score_new[lines, :1]
        highest = jnp.maximum(jnp.max(old, axis=-1, keepdims=True), new)
        weight_old = jnp.exp(old - highest)
        weight_new = jnp.exp(new - highest)
        denominator = jnp.sum(weight_old, axis=-1, keepdims=True) + weight_new
        scores[lines, :] = weight_old / denominator
        weight_new = (weight_new / denominator).astype(jnp.bfloat16).astype(jnp.float32)
        values_new[lines, :] = values_new[lines, :] * weight_new

        for index in range(live):
            at = slice(first_line + index * slot, first_line + (index + 1) * slot)
            mixed = jnp.dot(
                scores[at, :].astype(jnp.bfloat16), vc[row_of(batch, index)],
                preferred_element_type=jnp.float32,
            )
            taken = mixed[:, :HEAD_DIM]
            for kv in range(1, kv_local):
                taken = jnp.where(
                    head_of == kv, mixed[:, kv * HEAD_DIM : (kv + 1) * HEAD_DIM], taken
                )
            attended[at, :] = taken + values_new[at, :]

        flat = jnp.concatenate(
            [
                attended[pl.ds(first_line + head, PADDED, stride=slot), :].astype(jnp.bfloat16)
                for head in range(heads)
            ],
            axis=1,
        )

        if batch == 0:
            loads["wo"].wait()

        @pl.when(inner)
        def _():
            if batch == 0:
                pl.semaphore_wait(barrier, chips)
            send_before(stage).start()

        def project(order):
            parity, at = (1 - core, order) if order < chips else (core, order - chips)
            start = jnp.where(last, closing[order], 2 * at + parity) * width
            columns = pl.ds(pl.multiple_of(start, width), width)
            return jnp.dot(flat, wo[:, columns], preferred_element_type=jnp.float32)

        part, part_in, chip_sum = stage["part"], stage["part_in"], stage["chip_sum"]
        direct = stage["direct"]
        tail = None
        for order in range(chips):
            product = project(order)
            direct[order] = product.astype(jnp.bfloat16)
            part[order] = product[:TILE, :].astype(jnp.bfloat16)
            if order % 2 == 0:
                tail = product[TILE:, :]
            else:
                part[chips + order // 2] = pack(tail, product[TILE:, :]).astype(jnp.bfloat16)

            @pl.when(last)
            def _():
                send_direct(stage, order).start()

            if order + 1 in (chips // 2, chips):
                @pl.when(inner)
                def _():
                    send_part(stage, 0 if order + 1 < chips else 1).start()

        mine = [project(order) for order in range(chips, tensors)]

        @pl.when(last)
        def _():
            for order in range(chips, tensors - 1):
                direct[order] = mine[order - chips].astype(jnp.bfloat16)
                send_direct(stage, order).start()
            final[batch] = mine[-1]

        @pl.when(inner)
        def _():
            for piece, (first, end) in enumerate(pieces):
                send_part(stage, piece).wait_recv()
                for block in range(first, end):
                    if block < chips:
                        own_sum = mine[block][:TILE, :]
                    else:
                        pair = 2 * (block - chips)
                        own_sum = pack(mine[pair][TILE:, :], mine[pair + 1][TILE:, :])
                    chip_sum[block] = (
                        own_sum + part_in[block].astype(jnp.float32)
                    ).astype(jnp.bfloat16)
                for step in range(1, chips + 1):
                    send_sum(stage, lax.rem(chip + step, chips), piece).start()
            for at in range(chips):
                @pl.when(chip != at)
                def _():
                    for which in range(2):
                        send_owned(stage, at, which).start()

    odd = lax.rem(chip, 2) == 1

    def finish(batch):
        stage = stages[batch]

        @pl.when(last)
        def _():
            total = final[batch]
            for off in range(1, tensors):
                other = lax.rem(me + off, tensors)
                arrived = stage["direct_in"].at[other]
                remote(
                    arrived, arrived, stage["direct_send"].at[off - 1],
                    stage["direct_recv"].at[other], sibling,
                ).wait_recv()
                total = total + arrived[...].astype(jnp.float32)
            final[batch] = total

        @pl.when(inner)
        def _():
            owned_in, chip_sum = stage["owned_in"], stage["chip_sum"]
            owned_in[chip, 0] = chip_sum[chip]
            owned_in[chip, 1] = chip_sum[chips + chip // 2]
            totals = [jnp.zeros((TILE, width), jnp.float32) for _ in range(2)]
            for source in range(chips):
                @pl.when(chip != source)
                def _():
                    for which in range(2):
                        arrived = owned_in.at[source, which]
                        remote(
                            arrived, arrived, stage["owned_send"].at[source, which],
                            stage["owned_recv"].at[source, which], sibling,
                        ).wait_recv()

                for which in range(2):
                    totals[which] = totals[which] + owned_in[source, which].astype(jnp.float32)
            final[batch, :TILE, :] = totals[0]
            final[batch, TILE:, :] = jnp.where(odd, turn(totals[1]), totals[1])

        hid = stage["hid"]
        wide = hid[core, chip].astype(jnp.float32)
        main_on = running[0, batch, :TILE, :1]
        main = wide + main_on * final[batch, :TILE, :]
        out_hidden[0, batch * TILE : (batch + 1) * TILE, :] = main.astype(jnp.bfloat16)
        wide = hid[core, chips + chip // 2].astype(jnp.float32)
        wide = jnp.where(odd, turn(wide), wide)
        return wide + running[0, batch, TILE:, :1] * final[batch, TILE:, :]

    for batch in batches:
        receive(batch)
        compute(batch)
    tails = slice(2 * TILE, 3 * TILE)
    for target, held in ((out_keys, tail_keys), (out_values, tail_values)):
        columns = held.shape[2]
        for start in range(0, columns, min(columns, width)):
            at = slice(start, start + min(columns, width))
            packed = pack(held[0, :, at], held[1, :, at])
            target[0, tails, at] = packed.astype(jnp.bfloat16)
    out_hidden[0, tails, :] = pack(finish(0), finish(1)).astype(jnp.bfloat16)

    for stage in stages:
        @pl.when(section == 0)
        def _():
            for off in range(1, tensors):
                entering(stage, off).wait_send()

        @pl.when(section > 0)
        def _():
            for piece in range(len(pieces)):
                swap_half(stage, core, piece).wait_send()

        @pl.when(last)
        def _():
            for order in range(tensors - 1):
                send_direct(stage, order).wait_send()

        @pl.when(inner)
        def _():
            send_before(stage).wait_send()
            for piece in range(len(pieces)):
                send_part(stage, piece).wait_send()
                for target in range(chips):
                    send_sum(stage, target, piece).wait_send()
            for at in range(chips):
                @pl.when(chip != at)
                def _():
                    for which in range(2):
                        send_owned(stage, at, which).wait_send()


def emit_kernel(hidden_ref, keys_ref, values_ref, out_hidden, out_keys, out_values):
    out_hidden[...] = hidden_ref[...]
    out_keys[...] = keys_ref[...]
    out_values[...] = values_ref[...]


def solution(mesh):
    sections = mesh.shape["section"]
    tensors = mesh.shape["tensor"]
    chips = tensors // 2

    def per_device(
        inputs, gains, w_query, w_key, w_value, w_out, key_cache, value_cache, cache_lens, exit_plan
    ):
        rows, width = inputs.shape
        features = gains.shape[1]
        query_width = w_query.shape[2]
        kv_width = w_key.shape[2]
        heads = query_width // HEAD_DIM
        groups_per_kv = query_width // kv_width
        slot = -(-heads // 8) * 8
        slots = key_cache.shape[2]
        any_spec = pl.BlockSpec(memory_space=pl.ANY)
        vmem_spec = pl.BlockSpec(memory_space=pltpu.VMEM)
        bf16, f32 = jnp.bfloat16, jnp.float32
        batches = 2
        lines = batches * PADDED * slot
        blocks = chips + chips // 2

        def stage_scratch(batch):
            def vmem(*shape):
                return pltpu.VMEM((*shape, width), bf16)

            def sems(*shape):
                return pltpu.SemaphoreType.DMA(shape)

            return dict(
                enter=vmem(2, chips, PADDED if batch == 0 else TILE),
                hid=vmem(2, blocks, TILE), before=vmem(blocks, TILE), part=vmem(blocks, TILE),
                part_in=vmem(blocks, TILE), chip_sum=vmem(blocks, TILE),
                sums_in=vmem(chips, blocks, TILE), owned_in=vmem(chips, 2, TILE),
                direct=vmem(tensors - 1, PADDED), direct_in=vmem(tensors, PADDED),
                enter_send=sems(tensors), enter_recv=sems(2, chips),
                half_send=sems(2), half_recv=sems(2), before_send=sems(1),
                before_recv=sems(1), part_send=sems(2), part_recv=sems(2),
                sums_send=sems(chips, 2), sums_recv=sems(chips, 2),
                owned_send=sems(chips, 2), owned_recv=sems(chips, 2),
                direct_send=sems(tensors - 1), direct_recv=sems(tensors),
            )

        results = pl.pallas_call(
            functools.partial(relay_kernel, sections, tensors, groups_per_kv),
            out_shape=(
                jax.ShapeDtypeStruct((1, rows, width), bf16),
                jax.ShapeDtypeStruct((1, rows, kv_width), bf16),
                jax.ShapeDtypeStruct((1, rows, kv_width), bf16),
            ),
            in_specs=[any_spec] * 10,
            out_specs=(vmem_spec,) * 3,
            scratch_shapes=[
                pltpu.VMEM((features, query_width), bf16),
                pltpu.VMEM((features, kv_width), bf16),
                pltpu.VMEM((features, kv_width), bf16),
                pltpu.VMEM((query_width, features), bf16),
                pltpu.VMEM((rows, slots, kv_width), bf16),
                pltpu.VMEM((rows, slots, kv_width), bf16),
                pltpu.VMEM((1, features), f32),
                pltpu.VMEM((rows, width), bf16),
                pltpu.VMEM((PADDED, features), bf16),
                pltpu.VMEM((batches, PADDED, HEAD_DIM), f32),
                pltpu.VMEM((2, batches, PADDED, HEAD_DIM), f32),
                pltpu.VMEM((lines, slots), f32),
                pltpu.VMEM((lines, HEAD_DIM), f32),
                pltpu.VMEM((lines, slots), f32),
                pltpu.VMEM((lines, HEAD_DIM), f32),
                pltpu.VMEM((lines, HEAD_DIM), f32),
                pltpu.VMEM((lines, HEAD_DIM), f32),
                pltpu.VMEM((batches, PADDED, width), f32),
                pltpu.VMEM((batches, TILE, kv_width), f32),
                pltpu.VMEM((batches, TILE, kv_width), f32),
                pltpu.SMEM((rows,), jnp.int32),
                pltpu.SMEM((rows,), jnp.int32),
                pltpu.SemaphoreType.DMA((10,)),
                tuple(stage_scratch(batch) for batch in range(batches)),
            ],
            compiler_params=pltpu.CompilerParams(
                collective_id=0, has_side_effects=True, vmem_limit_bytes=48 * 1024 * 1024
            ),
            name="relay",
        )(
            *(
                pltpu.with_memory_space_constraint(array, pltpu.HBM)
                for array in (
                    cache_lens, exit_plan, inputs, gains, w_query, w_key, w_value, w_out,
                    key_cache, value_cache,
                )
            )
        )
        return pl.pallas_call(
            emit_kernel,
            out_shape=tuple(jax.ShapeDtypeStruct(r.shape, r.dtype) for r in results),
            in_specs=[vmem_spec] * 3,
            out_specs=(vmem_spec,) * 3,
            compiler_params=pltpu.CompilerParams(vmem_limit_bytes=1024 * 1024),
            name="emit",
        )(*results)

    return jax.shard_map(
        per_device,
        mesh=mesh,
        in_specs=(
            P("group", "tensor"),
            P("section", None),
            P("section", None, "tensor"),
            P("section", None, "tensor"),
            P("section", None, "tensor"),
            P("section", "tensor", None),
            P("section", "group", None, "tensor"),
            P("section", "group", None, "tensor"),
            P("group"),
            P("group"),
        ),
        out_specs=(
            P("section", "group", "tensor"),
            P("section", "group", "tensor"),
            P("section", "group", "tensor"),
        ),
        check_vma=False,
    )
```

```python
import functools
import math

import jax
import jax.numpy as jnp
from jax import lax
from jax.experimental import pallas as pl
from jax.experimental.pallas import tpu as pltpu
from jax.sharding import PartitionSpec as P

HEAD_DIM = 128
NORM_EPSILON = 1e-05
ROPE_BASE = 500000.0
MASKED_SCORE = -1e30
MESH = pl.DeviceIdType.MESH


HALF_TILE = 4
TILE = 8
PADDED = 16


def row_of(batch, index):
    if index < TILE:
        return batch * TILE + index
    return 2 * TILE + HALF_TILE * batch + (index - TILE) % HALF_TILE


def relay_kernel(
    sections, tensors, groups_per_kv,
    lens_ref, plan_ref, inputs_ref, gains_ref, wq_ref, wk_ref, wv_ref, wo_ref, kc_ref, vc_ref,
    out_hidden, out_keys, out_values,
    wq, wk, wv, wo, kc, vc, gain, own, normed,
    pos, running, mask, queries, scores, score_new, values_new, attended,
    final, tail_keys, tail_values,
    lens, plan, load_sem, stages,
):
    width = own.shape[1]
    live = TILE + HALF_TILE
    batches = range(len(stages))
    chips = tensors // 2
    blocks = chips + chips // 2
    pieces = ((0, chips // 2), (chips // 2, blocks))
    kv_local = wk.shape[1] // HEAD_DIM
    heads = kv_local * groups_per_kv
    slot = queries.shape[0] // (PADDED * len(stages))
    slots = kc.shape[1]
    section = lax.axis_index("section")
    me = lax.axis_index("tensor")
    chip = me // 2
    core = lax.rem(me, 2)
    sibling = {"tensor": 2 * chip + 1 - core}
    inner = section < sections - 1
    last = section == sections - 1

    def load(source, target, index):
        return pltpu.make_async_copy(source, target, load_sem.at[index])

    def remote(source, target, send_sem, recv_sem, device):
        return pltpu.make_async_remote_copy(
            src_ref=source, dst_ref=target, send_sem=send_sem, recv_sem=recv_sem,
            device_id=device, device_id_type=MESH,
        )

    loads = dict(
        gain=load(gains_ref, gain, 0),
        wk=load(wk_ref.at[0], wk, 1),
        wv=load(wv_ref.at[0], wv, 2),
        wq=load(wq_ref.at[0], wq, 3),
        kc=load(kc_ref.at[0], kc, 4),
        vc=load(vc_ref.at[0], vc, 5),
        wo=load(wo_ref.at[0], wo, 6),
        lens=load(lens_ref, lens, 8),
        plan=load(plan_ref, plan, 9),
    )
    own_entering = load(inputs_ref, own, 7)

    @pl.when(section == 0)
    def _():
        own_entering.start()

    for name in ("lens", "plan", "gain", "wk", "wv", "wq", "kc", "vc", "wo"):
        loads[name].start()

    barrier = pltpu.get_barrier_semaphore()

    def greet(device):
        pl.semaphore_signal(barrier, inc=1, device_id=device, device_id_type=MESH)

    for off in range(1, tensors):
        greet({"tensor": lax.rem(me + off, tensors)})

    pl.semaphore_wait(barrier, (tensors - 1) + chips * (section > 0).astype(jnp.int32))

    @pl.when(section > 0)
    def _():
        for other in range(chips):
            greet({"section": section - 1, "tensor": 2 * other + core})

    @pl.when(inner)
    def _():
        for other in range(chips):
            greet({"section": section + 1, "tensor": 2 * other + core})

    def entering(stage, off):
        return remote(
            stage["enter"].at[core, chip], stage["enter"].at[core, chip],
            stage["enter_send"].at[off], stage["enter_recv"].at[core, chip],
            {"tensor": lax.rem(me + off, tensors)},
        )

    def span_of(piece):
        first, end = pieces[piece]
        return pl.ds(first, end - first)

    def swap_half(stage, parity, piece):
        part_of = stage["hid"].at[parity, span_of(piece)]
        return remote(
            part_of, part_of, stage["half_send"].at[piece], stage["half_recv"].at[piece], sibling
        )

    def send_sum(stage, target, piece):
        return remote(
            stage["chip_sum"].at[span_of(piece)], stage["sums_in"].at[chip, span_of(piece)],
            stage["sums_send"].at[target, piece], stage["sums_recv"].at[chip, piece],
            {"section": section + 1, "tensor": 2 * target + core},
        )

    def send_before(stage):
        return remote(
            stage["hid"].at[core], stage["before"], stage["before_send"].at[0],
            stage["before_recv"].at[0], {"section": section + 1},
        )

    def send_part(stage, piece):
        return remote(
            stage["part"].at[span_of(piece)], stage["part_in"].at[span_of(piece)],
            stage["part_send"].at[piece], stage["part_recv"].at[piece], sibling,
        )

    def send_owned(stage, at, which):
        block = at if which == 0 else chips + at // 2
        return remote(
            stage["chip_sum"].at[block], stage["owned_in"].at[chip, which],
            stage["owned_send"].at[at, which], stage["owned_recv"].at[chip, which],
            {"tensor": 2 * at + core},
        )

    closing = []
    for step in range(1, chips):
        other = lax.rem(chip + step, chips)
        closing += [2 * other + core, 2 * other + 1 - core]
    closing += [2 * chip + 1 - core, me]

    def send_direct(stage, order):
        return remote(
            stage["direct"].at[order], stage["direct_in"].at[me],
            stage["direct_send"].at[order], stage["direct_recv"].at[me],
            {"tensor": closing[order]},
        )

    @pl.when(section == 0)
    def _():
        own_entering.wait()
        stages[0]["enter"][core, chip, :TILE, :] = own[:TILE, :]
        stages[0]["enter"][core, chip, TILE:, :] = own[2 * TILE :, :]
        stages[1]["enter"][core, chip] = own[TILE : 2 * TILE, :]
        for stage in stages:
            for off in range(1, tensors):
                entering(stage, off).start()

    for name in ("lens", "plan"):
        loads[name].wait()
    lane = lax.broadcasted_iota(jnp.int32, (slot, slots), 1)
    for batch in batches:
        for index in range(PADDED):
            row = row_of(batch, index)
            length = lens[row]
            place = slice(index, index + 1)
            pos[batch, place, :] = jnp.full((1, HEAD_DIM), length, jnp.int32).astype(jnp.float32)
            planned = jnp.full((1, HEAD_DIM), plan[row], jnp.int32)
            running[0, batch, place, :] = (planned > section).astype(jnp.float32)
            running[1, batch, place, :] = (planned > section - 1).astype(jnp.float32)
            if index < live:
                line = (batch * PADDED + index) * slot
                mask[line : line + slot, :] = (lane < length).astype(jnp.float32)
    half_lane = lax.broadcasted_iota(jnp.int32, (PADDED, HEAD_DIM), 1)
    half = HEAD_DIM // 2
    step_at = jnp.where(half_lane < half, half_lane, half_lane - half).astype(jnp.float32)
    frequency = jnp.exp(step_at * (-2.0 * math.log(ROPE_BASE) / HEAD_DIM))
    turns = []
    for batch in batches:
        angles = pos[batch] * frequency
        sin_part = jnp.sin(angles)
        turns.append((jnp.cos(angles), jnp.where(half_lane < half, -sin_part, sin_part)))
    attended[...] = jnp.zeros_like(attended)
    if heads < slot:
        queries[...] = jnp.zeros_like(queries)
        score_new[...] = jnp.zeros_like(score_new)
        values_new[...] = jnp.zeros_like(values_new)

    upper = lax.broadcasted_iota(jnp.int32, (TILE, width), 0) < HALF_TILE

    def turn(block):
        return pltpu.roll(block, HALF_TILE, 0)

    def pack(first, second):
        return jnp.where(upper[:, : first.shape[1]], first, turn(second))

    def take_entering(batch):
        stage = stages[batch]
        hid = stage["hid"]

        @pl.when(section == 0)
        def _():
            enter, shared = stage["enter"], stages[0]["enter"]
            for off in range(1, tensors):
                other = lax.rem(me + off, tensors)
                at = (lax.rem(other, 2), other // 2)
                remote(
                    enter.at[at], enter.at[at], stage["enter_send"].at[off],
                    stage["enter_recv"].at[at], sibling,
                ).wait_recv()
            for parity in range(2):
                for at in range(chips):
                    hid[parity, at] = enter[parity, at, :TILE, :]
                for pair in range(chips // 2):
                    tails = [
                        shared[parity, 2 * pair + side, TILE:, :].astype(jnp.float32)
                        for side in range(2)
                    ]
                    if batch == 0:
                        packed = jnp.where(upper, tails[0], turn(tails[1]))
                    else:
                        packed = jnp.where(upper, turn(tails[0]), tails[1])
                    hid[parity, chips + pair] = packed.astype(jnp.bfloat16)

    def receive(batch):
        stage = stages[batch]
        hid = stage["hid"]

        @pl.when(section > 0)
        def _():
            before, sums_in = stage["before"], stage["sums_in"]
            remote(
                before, before, stage["before_send"].at[0], stage["before_recv"].at[0],
                {"section": section - 1},
            ).wait_recv()
            for piece, (first, end) in enumerate(pieces):
                for source in range(chips):
                    arrived = sums_in.at[source, span_of(piece)]
                    remote(
                        arrived, arrived, stage["sums_send"].at[source, piece],
                        stage["sums_recv"].at[source, piece], {"section": section - 1},
                    ).wait_recv()
                for block in range(first, end):
                    total = jnp.zeros((TILE, width), jnp.float32)
                    for source in range(chips):
                        total = total + sums_in[source, block].astype(jnp.float32)
                    wide = before[block].astype(jnp.float32)
                    rows_on = slice(0, TILE) if block < chips else slice(TILE, PADDED)
                    on = running[1, batch, rows_on, :1]
                    hid[core, block] = (wide + on * total).astype(jnp.bfloat16)
                swap_half(stage, core, piece).start()
            for piece in range(len(pieces)):
                swap_half(stage, 1 - core, piece).wait_recv()

    inv_root = 1.0 / math.sqrt(HEAD_DIM)
    head_of = lax.broadcasted_iota(jnp.int32, (slot, HEAD_DIM), 0) // groups_per_kv

    def compute(batch):
        stage = stages[batch]
        hid = stage["hid"]
        cos_here, sin_here = turns[batch]
        first_line = batch * PADDED * slot

        def rotate(vectors):
            return vectors * cos_here + pltpu.roll(vectors, half, 1) * sin_here

        if batch == 0:
            for name in ("gain", "wk", "wv", "wq", "kc", "vc"):
                loads[name].wait()

        squares = jnp.zeros((TILE, 1), jnp.float32)
        tail_squares = jnp.zeros((TILE, 1), jnp.float32)
        for parity in range(2):
            for block in range(blocks):
                wide = hid[parity, block].astype(jnp.float32)
                square = jnp.sum(wide * wide, axis=-1, keepdims=True)
                if block < chips:
                    squares = squares + square
                else:
                    tail_squares = tail_squares + square
        tail_squares = jnp.broadcast_to(tail_squares, (TILE, HEAD_DIM))
        tail_squares = (tail_squares + turn(tail_squares))[:, :1]
        scale = lax.rsqrt(squares / (tensors * width) + NORM_EPSILON)
        tail_scale = lax.rsqrt(tail_squares / (tensors * width) + NORM_EPSILON)
        for parity in range(2):
            for pair in range(chips // 2):
                columns = [
                    slice((2 * at + parity) * width, (2 * at + parity + 1) * width)
                    for at in (2 * pair, 2 * pair + 1)
                ]
                gains = [jnp.broadcast_to(gain[:, at], (TILE, width)) for at in columns]
                tail = hid[parity, chips + pair].astype(jnp.float32)
                tail = tail * tail_scale * jnp.where(upper, gains[0], gains[1])
                for side, at in enumerate(columns):
                    wide = hid[parity, 2 * pair + side].astype(jnp.float32)
                    wide = wide * scale * gains[side]
                    both = jnp.concatenate([wide, tail if side == 0 else turn(tail)], axis=0)
                    normed[:, at] = both.astype(jnp.bfloat16)

        entered = normed[...]
        key_new = jnp.dot(entered, wk[...], preferred_element_type=jnp.float32)
        value_new = jnp.dot(entered, wv[...], preferred_element_type=jnp.float32)
        tail_values[batch] = value_new[TILE:, :]
        value_new = value_new.astype(jnp.bfloat16)
        main_rows = slice(batch * TILE, (batch + 1) * TILE)
        out_values[0, main_rows, :] = value_new[:TILE, :]
        keys = []
        values = []
        for kv in range(kv_local):
            at = slice(kv * HEAD_DIM, (kv + 1) * HEAD_DIM)
            rotated = rotate(key_new[:, at])
            tail_keys[batch, :, at] = rotated[TILE:, :]
            rotated = rotated.astype(jnp.bfloat16)
            out_keys[0, main_rows, at] = rotated[:TILE, :]
            keys.append(rotated.astype(jnp.float32))
            values.append(value_new[:, at].astype(jnp.float32))

        tile = min(256, heads * HEAD_DIM)
        for start in range(0, heads * HEAD_DIM, tile):
            product = jnp.dot(
                entered, wq[:, start : start + tile], preferred_element_type=jnp.float32
            )
            for side in range(tile // HEAD_DIM):
                head = start // HEAD_DIM + side
                kv = head // groups_per_kv
                query = rotate(product[:, side * HEAD_DIM : (side + 1) * HEAD_DIM])
                query = query.astype(jnp.bfloat16).astype(jnp.float32)
                at = pl.ds(first_line + head, PADDED, stride=slot)
                queries[at, :] = query
                score = jnp.sum(query * keys[kv], axis=-1, keepdims=True) * inv_root
                score_new[at, :] = jnp.broadcast_to(score, (PADDED, HEAD_DIM))
                values_new[at, :] = values[kv]

        for index in range(live):
            at = slice(first_line + index * slot, first_line + (index + 1) * slot)
            query = queries[at, :]
            spread = jnp.concatenate(
                [jnp.where(head_of == kv, query, 0.0) for kv in range(kv_local)], axis=1
            ).astype(jnp.bfloat16)
            scores[at, :] = lax.dot_general(
                spread, kc[row_of(batch, index)], (((1,), (1,)), ((), ())),
                preferred_element_type=jnp.float32,
            )

        lines = slice(first_line, first_line + live * slot)
        old = jnp.where(mask[lines, :] > 0.0, scores[lines, :] * inv_root, MASKED_SCORE)
        new = score_new[lines, :1]
        highest = jnp.maximum(jnp.max(old, axis=-1, keepdims=True), new)
        weight_old = jnp.exp(old - highest)
        weight_new = jnp.exp(new - highest)
        denominator = jnp.sum(weight_old, axis=-1, keepdims=True) + weight_new
        scores[lines, :] = weight_old / denominator
        weight_new = (weight_new / denominator).astype(jnp.bfloat16).astype(jnp.float32)
        values_new[lines, :] = values_new[lines, :] * weight_new

        for index in range(live):
            at = slice(first_line + index * slot, first_line + (index + 1) * slot)
            mixed = jnp.dot(
                scores[at, :].astype(jnp.bfloat16), vc[row_of(batch, index)],
                preferred_element_type=jnp.float32,
            )
            taken = mixed[:, :HEAD_DIM]
            for kv in range(1, kv_local):
                taken = jnp.where(
                    head_of == kv, mixed[:, kv * HEAD_DIM : (kv + 1) * HEAD_DIM], taken
                )
            attended[at, :] = taken + values_new[at, :]

        flat = jnp.concatenate(
            [
                attended[pl.ds(first_line + head, PADDED, stride=slot), :].astype(jnp.bfloat16)
                for head in range(heads)
            ],
            axis=1,
        )

        if batch == 0:
            loads["wo"].wait()

        @pl.when(inner)
        def _():
            if batch == 0:
                pl.semaphore_wait(barrier, chips)
            send_before(stage).start()

        def project(order):
            parity, at = (1 - core, order) if order < chips else (core, order - chips)
            start = jnp.where(last, closing[order], 2 * at + parity) * width
            columns = pl.ds(pl.multiple_of(start, width), width)
            return jnp.dot(flat, wo[:, columns], preferred_element_type=jnp.float32)

        part, part_in, chip_sum = stage["part"], stage["part_in"], stage["chip_sum"]
        direct = stage["direct"]
        tail = None
        for order in range(chips):
            product = project(order)
            part[order] = product[:TILE, :].astype(jnp.bfloat16)
            if order % 2 == 0:
                tail = product[TILE:, :]
            else:
                part[chips + order // 2] = pack(tail, product[TILE:, :]).astype(jnp.bfloat16)

            @pl.when(last)
            def _():
                direct[order] = product.astype(jnp.bfloat16)
                send_direct(stage, order).start()

            if order + 1 in (chips // 2, chips):
                @pl.when(inner)
                def _():
                    send_part(stage, 0 if order + 1 < chips else 1).start()

        mine = [project(order) for order in range(chips, tensors)]

        @pl.when(last)
        def _():
            for order in range(chips, tensors - 1):
                direct[order] = mine[order - chips].astype(jnp.bfloat16)
                send_direct(stage, order).start()
            final[batch] = mine[-1]

        @pl.when(inner)
        def _():
            for piece, (first, end) in enumerate(pieces):
                send_part(stage, piece).wait_recv()
                for block in range(first, end):
                    if block < chips:
                        own_sum = mine[block][:TILE, :]
                    else:
                        pair = 2 * (block - chips)
                        own_sum = pack(mine[pair][TILE:, :], mine[pair + 1][TILE:, :])
                    chip_sum[block] = (
                        own_sum + part_in[block].astype(jnp.float32)
                    ).astype(jnp.bfloat16)
                for step in range(1, chips + 1):
                    send_sum(stage, lax.rem(chip + step, chips), piece).start()
            for at in range(chips):
                @pl.when(chip != at)
                def _():
                    for which in range(2):
                        send_owned(stage, at, which).start()

    odd = lax.rem(chip, 2) == 1

    def finish(batch):
        stage = stages[batch]

        @pl.when(last)
        def _():
            total = final[batch]
            for off in range(1, tensors):
                other = lax.rem(me + off, tensors)
                arrived = stage["direct_in"].at[other]
                remote(
                    arrived, arrived, stage["direct_send"].at[off - 1],
                    stage["direct_recv"].at[other], sibling,
                ).wait_recv()
                total = total + arrived[...].astype(jnp.float32)
            final[batch] = total

        @pl.when(inner)
        def _():
            owned_in, chip_sum = stage["owned_in"], stage["chip_sum"]
            owned_in[chip, 0] = chip_sum[chip]
            owned_in[chip, 1] = chip_sum[chips + chip // 2]
            totals = [jnp.zeros((TILE, width), jnp.float32) for _ in range(2)]
            for source in range(chips):
                @pl.when(chip != source)
                def _():
                    for which in range(2):
                        arrived = owned_in.at[source, which]
                        remote(
                            arrived, arrived, stage["owned_send"].at[source, which],
                            stage["owned_recv"].at[source, which], sibling,
                        ).wait_recv()

                for which in range(2):
                    totals[which] = totals[which] + owned_in[source, which].astype(jnp.float32)
            final[batch, :TILE, :] = totals[0]
            final[batch, TILE:, :] = jnp.where(odd, turn(totals[1]), totals[1])

        hid = stage["hid"]
        wide = hid[core, chip].astype(jnp.float32)
        main_on = running[0, batch, :TILE, :1]
        main = wide + main_on * final[batch, :TILE, :]
        out_hidden[0, batch * TILE : (batch + 1) * TILE, :] = main.astype(jnp.bfloat16)
        wide = hid[core, chips + chip // 2].astype(jnp.float32)
        wide = jnp.where(odd, turn(wide), wide)
        return wide + running[0, batch, TILE:, :1] * final[batch, TILE:, :]

    for batch in batches:
        take_entering(batch)
    for batch in batches:
        receive(batch)
        compute(batch)
    tails = slice(2 * TILE, 3 * TILE)
    for target, held in ((out_keys, tail_keys), (out_values, tail_values)):
        columns = held.shape[2]
        for start in range(0, columns, min(columns, width)):
            at = slice(start, start + min(columns, width))
            packed = pack(held[0, :, at], held[1, :, at])
            target[0, tails, at] = packed.astype(jnp.bfloat16)
    out_hidden[0, tails, :] = pack(finish(0), finish(1)).astype(jnp.bfloat16)

    for stage in stages:
        @pl.when(section == 0)
        def _():
            for off in range(1, tensors):
                entering(stage, off).wait_send()

        @pl.when(section > 0)
        def _():
            for piece in range(len(pieces)):
                swap_half(stage, core, piece).wait_send()

        @pl.when(last)
        def _():
            for order in range(tensors - 1):
                send_direct(stage, order).wait_send()

        @pl.when(inner)
        def _():
            send_before(stage).wait_send()
            for piece in range(len(pieces)):
                send_part(stage, piece).wait_send()
                for target in range(chips):
                    send_sum(stage, target, piece).wait_send()
            for at in range(chips):
                @pl.when(chip != at)
                def _():
                    for which in range(2):
                        send_owned(stage, at, which).wait_send()


def emit_kernel(hidden_ref, keys_ref, values_ref, out_hidden, out_keys, out_values):
    out_hidden[...] = hidden_ref[...]
    out_keys[...] = keys_ref[...]
    out_values[...] = values_ref[...]


def solution(mesh):
    sections = mesh.shape["section"]
    tensors = mesh.shape["tensor"]
    chips = tensors // 2

    def per_device(
        inputs, gains, w_query, w_key, w_value, w_out, key_cache, value_cache, cache_lens, exit_plan
    ):
        rows, width = inputs.shape
        features = gains.shape[1]
        query_width = w_query.shape[2]
        kv_width = w_key.shape[2]
        heads = query_width // HEAD_DIM
        groups_per_kv = query_width // kv_width
        slot = -(-heads // 8) * 8
        slots = key_cache.shape[2]
        any_spec = pl.BlockSpec(memory_space=pl.ANY)
        vmem_spec = pl.BlockSpec(memory_space=pltpu.VMEM)
        bf16, f32 = jnp.bfloat16, jnp.float32
        batches = 2
        lines = batches * PADDED * slot
        blocks = chips + chips // 2

        def stage_scratch(batch):
            def vmem(*shape):
                return pltpu.VMEM((*shape, width), bf16)

            def sems(*shape):
                return pltpu.SemaphoreType.DMA(shape)

            return dict(
                enter=vmem(2, chips, PADDED if batch == 0 else TILE),
                hid=vmem(2, blocks, TILE), before=vmem(blocks, TILE), part=vmem(blocks, TILE),
                part_in=vmem(blocks, TILE), chip_sum=vmem(blocks, TILE),
                sums_in=vmem(chips, blocks, TILE), owned_in=vmem(chips, 2, TILE),
                direct=vmem(tensors - 1, PADDED), direct_in=vmem(tensors, PADDED),
                enter_send=sems(tensors), enter_recv=sems(2, chips),
                half_send=sems(2), half_recv=sems(2), before_send=sems(1),
                before_recv=sems(1), part_send=sems(2), part_recv=sems(2),
                sums_send=sems(chips, 2), sums_recv=sems(chips, 2),
                owned_send=sems(chips, 2), owned_recv=sems(chips, 2),
                direct_send=sems(tensors - 1), direct_recv=sems(tensors),
            )

        results = pl.pallas_call(
            functools.partial(relay_kernel, sections, tensors, groups_per_kv),
            out_shape=(
                jax.ShapeDtypeStruct((1, rows, width), bf16),
                jax.ShapeDtypeStruct((1, rows, kv_width), bf16),
                jax.ShapeDtypeStruct((1, rows, kv_width), bf16),
            ),
            in_specs=[any_spec] * 10,
            out_specs=(vmem_spec,) * 3,
            scratch_shapes=[
                pltpu.VMEM((features, query_width), bf16),
                pltpu.VMEM((features, kv_width), bf16),
                pltpu.VMEM((features, kv_width), bf16),
                pltpu.VMEM((query_width, features), bf16),
                pltpu.VMEM((rows, slots, kv_width), bf16),
                pltpu.VMEM((rows, slots, kv_width), bf16),
                pltpu.VMEM((1, features), f32),
                pltpu.VMEM((rows, width), bf16),
                pltpu.VMEM((PADDED, features), bf16),
                pltpu.VMEM((batches, PADDED, HEAD_DIM), f32),
                pltpu.VMEM((2, batches, PADDED, HEAD_DIM), f32),
                pltpu.VMEM((lines, slots), f32),
                pltpu.VMEM((lines, HEAD_DIM), f32),
                pltpu.VMEM((lines, slots), f32),
                pltpu.VMEM((lines, HEAD_DIM), f32),
                pltpu.VMEM((lines, HEAD_DIM), f32),
                pltpu.VMEM((lines, HEAD_DIM), f32),
                pltpu.VMEM((batches, PADDED, width), f32),
                pltpu.VMEM((batches, TILE, kv_width), f32),
                pltpu.VMEM((batches, TILE, kv_width), f32),
                pltpu.SMEM((rows,), jnp.int32),
                pltpu.SMEM((rows,), jnp.int32),
                pltpu.SemaphoreType.DMA((10,)),
                tuple(stage_scratch(batch) for batch in range(batches)),
            ],
            compiler_params=pltpu.CompilerParams(
                collective_id=0, has_side_effects=True, vmem_limit_bytes=48 * 1024 * 1024
            ),
            name="relay",
        )(
            *(
                pltpu.with_memory_space_constraint(array, pltpu.HBM)
                for array in (
                    cache_lens, exit_plan, inputs, gains, w_query, w_key, w_value, w_out,
                    key_cache, value_cache,
                )
            )
        )
        return pl.pallas_call(
            emit_kernel,
            out_shape=tuple(jax.ShapeDtypeStruct(r.shape, r.dtype) for r in results),
            in_specs=[vmem_spec] * 3,
            out_specs=(vmem_spec,) * 3,
            compiler_params=pltpu.CompilerParams(vmem_limit_bytes=1024 * 1024),
            name="emit",
        )(*results)

    return jax.shard_map(
        per_device,
        mesh=mesh,
        in_specs=(
            P("group", "tensor"),
            P("section", None),
            P("section", None, "tensor"),
            P("section", None, "tensor"),
            P("section", None, "tensor"),
            P("section", "tensor", None),
            P("section", "group", None, "tensor"),
            P("section", "group", None, "tensor"),
            P("group"),
            P("group"),
        ),
        out_specs=(
            P("section", "group", "tensor"),
            P("section", "group", "tensor"),
            P("section", "group", "tensor"),
        ),
        check_vma=False,
    )
```

```python
import functools
import math

import jax
import jax.numpy as jnp
from jax import lax
from jax.experimental import pallas as pl
from jax.experimental.pallas import tpu as pltpu
from jax.sharding import PartitionSpec as P

HEAD_DIM = 128
NORM_EPSILON = 1e-05
ROPE_BASE = 500000.0
MASKED_SCORE = -1e30
MESH = pl.DeviceIdType.MESH


HALF_TILE = 4
TILE = 8
PADDED = 16


def row_of(batch, index):
    if index < TILE:
        return batch * TILE + index
    return 2 * TILE + HALF_TILE * batch + (index - TILE) % HALF_TILE


def relay_kernel(
    sections, tensors, groups_per_kv,
    lens_ref, plan_ref, inputs_ref, gains_ref, wq_ref, wk_ref, wv_ref, wo_ref, kc_ref, vc_ref,
    out_hidden, out_keys, out_values,
    wq, wk, wv, wo, kc, vc, gain, own, normed,
    pos, running, mask, queries, scores, score_new, values_new, attended,
    final, tail_keys, tail_values,
    lens, plan, load_sem, stages,
):
    width = own.shape[1]
    live = TILE + HALF_TILE
    batches = range(len(stages))
    chips = tensors // 2
    blocks = chips + chips // 2
    pieces = ((0, chips // 2), (chips // 2, blocks))
    kv_local = wk.shape[1] // HEAD_DIM
    heads = kv_local * groups_per_kv
    slot = queries.shape[0] // (PADDED * len(stages))
    slots = kc.shape[1]
    section = lax.axis_index("section")
    me = lax.axis_index("tensor")
    chip = me // 2
    core = lax.rem(me, 2)
    sibling = {"tensor": 2 * chip + 1 - core}
    inner = section < sections - 1
    last = section == sections - 1

    def load(source, target, index):
        return pltpu.make_async_copy(source, target, load_sem.at[index])

    def remote(source, target, send_sem, recv_sem, device):
        return pltpu.make_async_remote_copy(
            src_ref=source, dst_ref=target, send_sem=send_sem, recv_sem=recv_sem,
            device_id=device, device_id_type=MESH,
        )

    loads = dict(
        gain=load(gains_ref, gain, 0),
        wk=load(wk_ref.at[0], wk, 1),
        wv=load(wv_ref.at[0], wv, 2),
        wq=load(wq_ref.at[0], wq, 3),
        kc=load(kc_ref.at[0], kc, 4),
        vc=load(vc_ref.at[0], vc, 5),
        wo=load(wo_ref.at[0], wo, 6),
        lens=load(lens_ref, lens, 8),
        plan=load(plan_ref, plan, 9),
    )
    own_entering = load(inputs_ref, own, 7)

    @pl.when(section == 0)
    def _():
        own_entering.start()

    for name in ("lens", "plan", "gain", "wk", "wv", "wq", "kc", "vc", "wo"):
        loads[name].start()

    barrier = pltpu.get_barrier_semaphore()

    def greet(device):
        pl.semaphore_signal(barrier, inc=1, device_id=device, device_id_type=MESH)

    for off in range(1, tensors):
        greet({"tensor": lax.rem(me + off, tensors)})

    pl.semaphore_wait(barrier, (tensors - 1) + chips * (section > 0).astype(jnp.int32))

    @pl.when(section > 0)
    def _():
        for other in range(chips):
            greet({"section": section - 1, "tensor": 2 * other + core})

    @pl.when(inner)
    def _():
        for other in range(chips):
            greet({"section": section + 1, "tensor": 2 * other + core})

    def entering(stage, off):
        return remote(
            stage["enter"].at[core, chip], stage["enter"].at[core, chip],
            stage["enter_send"].at[off], stage["enter_recv"].at[core, chip],
            {"tensor": lax.rem(me + off, tensors)},
        )

    def span_of(piece):
        first, end = pieces[piece]
        return pl.ds(first, end - first)

    def swap_half(stage, parity, piece):
        part_of = stage["hid"].at[parity, span_of(piece)]
        return remote(
            part_of, part_of, stage["half_send"].at[piece], stage["half_recv"].at[piece], sibling
        )

    def send_sum(stage, target, piece):
        return remote(
            stage["chip_sum"].at[span_of(piece)], stage["sums_in"].at[chip, span_of(piece)],
            stage["sums_send"].at[target, piece], stage["sums_recv"].at[chip, piece],
            {"section": section + 1, "tensor": 2 * target + core},
        )

    def send_before(stage):
        return remote(
            stage["hid"].at[core], stage["before"], stage["before_send"].at[0],
            stage["before_recv"].at[0], {"section": section + 1},
        )

    def send_part(stage, piece):
        return remote(
            stage["part"].at[span_of(piece)], stage["part_in"].at[span_of(piece)],
            stage["part_send"].at[piece], stage["part_recv"].at[piece], sibling,
        )

    def send_owned(stage, at, which):
        block = at if which == 0 else chips + at // 2
        return remote(
            stage["chip_sum"].at[block], stage["owned_in"].at[chip, which],
            stage["owned_send"].at[at, which], stage["owned_recv"].at[chip, which],
            {"tensor": 2 * at + core},
        )

    closing = []
    for step in range(1, chips):
        other = lax.rem(chip + step, chips)
        closing += [2 * other + core, 2 * other + 1 - core]
    closing += [2 * chip + 1 - core, me]

    def send_direct(stage, order):
        return remote(
            stage["direct"].at[order], stage["direct_in"].at[me],
            stage["direct_send"].at[order], stage["direct_recv"].at[me],
            {"tensor": closing[order]},
        )

    @pl.when(section == 0)
    def _():
        own_entering.wait()
        stages[0]["enter"][core, chip, :TILE, :] = own[:TILE, :]
        stages[0]["enter"][core, chip, TILE:, :] = own[2 * TILE :, :]
        stages[1]["enter"][core, chip] = own[TILE : 2 * TILE, :]
        for stage in stages:
            for off in range(1, tensors):
                entering(stage, off).start()

    for name in ("lens", "plan"):
        loads[name].wait()
    lane = lax.broadcasted_iota(jnp.int32, (slot, slots), 1)
    for batch in batches:
        for index in range(PADDED):
            row = row_of(batch, index)
            length = lens[row]
            place = slice(index, index + 1)
            pos[batch, place, :] = jnp.full((1, HEAD_DIM), length, jnp.int32).astype(jnp.float32)
            planned = jnp.full((1, HEAD_DIM), plan[row], jnp.int32)
            running[0, batch, place, :] = (planned > section).astype(jnp.float32)
            running[1, batch, place, :] = (planned > section - 1).astype(jnp.float32)
            if index < live:
                line = (batch * PADDED + index) * slot
                mask[line : line + slot, :] = (lane < length).astype(jnp.float32)
    half_lane = lax.broadcasted_iota(jnp.int32, (PADDED, HEAD_DIM), 1)
    half = HEAD_DIM // 2
    step_at = jnp.where(half_lane < half, half_lane, half_lane - half).astype(jnp.float32)
    frequency = jnp.exp(step_at * (-2.0 * math.log(ROPE_BASE) / HEAD_DIM))
    turns = []
    for batch in batches:
        angles = pos[batch] * frequency
        sin_part = jnp.sin(angles)
        turns.append((jnp.cos(angles), jnp.where(half_lane < half, -sin_part, sin_part)))
    attended[...] = jnp.zeros_like(attended)
    if heads < slot:
        queries[...] = jnp.zeros_like(queries)
        score_new[...] = jnp.zeros_like(score_new)
        values_new[...] = jnp.zeros_like(values_new)

    upper = lax.broadcasted_iota(jnp.int32, (TILE, width), 0) < HALF_TILE

    def turn(block):
        return pltpu.roll(block, HALF_TILE, 0)

    def pack(first, second):
        return jnp.where(upper[:, : first.shape[1]], first, turn(second))

    def take_entering(batch):
        stage = stages[batch]
        hid = stage["hid"]

        @pl.when(section == 0)
        def _():
            enter, shared = stage["enter"], stages[0]["enter"]
            for off in range(1, tensors):
                other = lax.rem(me + off, tensors)
                at = (lax.rem(other, 2), other // 2)
                remote(
                    enter.at[at], enter.at[at], stage["enter_send"].at[off],
                    stage["enter_recv"].at[at], sibling,
                ).wait_recv()
            for parity in range(2):
                for at in range(chips):
                    hid[parity, at] = enter[parity, at, :TILE, :]
                for pair in range(chips // 2):
                    tails = [
                        shared[parity, 2 * pair + side, TILE:, :].astype(jnp.float32)
                        for side in range(2)
                    ]
                    if batch == 0:
                        packed = jnp.where(upper, tails[0], turn(tails[1]))
                    else:
                        packed = jnp.where(upper, turn(tails[0]), tails[1])
                    hid[parity, chips + pair] = packed.astype(jnp.bfloat16)

    def receive(batch):
        stage = stages[batch]
        hid = stage["hid"]

        @pl.when(section > 0)
        def _():
            before, sums_in = stage["before"], stage["sums_in"]
            remote(
                before, before, stage["before_send"].at[0], stage["before_recv"].at[0],
                {"section": section - 1},
            ).wait_recv()
            for piece, (first, end) in enumerate(pieces):
                for source in range(chips):
                    arrived = sums_in.at[source, span_of(piece)]
                    remote(
                        arrived, arrived, stage["sums_send"].at[source, piece],
                        stage["sums_recv"].at[source, piece], {"section": section - 1},
                    ).wait_recv()
                for block in range(first, end):
                    total = jnp.zeros((TILE, width), jnp.float32)
                    for source in range(chips):
                        total = total + sums_in[source, block].astype(jnp.float32)
                    wide = before[block].astype(jnp.float32)
                    rows_on = slice(0, TILE) if block < chips else slice(TILE, PADDED)
                    on = running[1, batch, rows_on, :1]
                    hid[core, block] = (wide + on * total).astype(jnp.bfloat16)
                swap_half(stage, core, piece).start()
    inv_root = 1.0 / math.sqrt(HEAD_DIM)
    head_of = lax.broadcasted_iota(jnp.int32, (slot, HEAD_DIM), 0) // groups_per_kv

    def compute(batch):
        stage = stages[batch]
        hid = stage["hid"]
        cos_here, sin_here = turns[batch]
        first_line = batch * PADDED * slot

        def rotate(vectors):
            return vectors * cos_here + pltpu.roll(vectors, half, 1) * sin_here

        squares = jnp.zeros((TILE, 1), jnp.float32)
        tail_squares = jnp.zeros((TILE, 1), jnp.float32)
        for parity in (core, 1 - core):
            if parity is not core:
                @pl.when(section > 0)
                def _():
                    for piece in range(len(pieces)):
                        swap_half(stage, parity, piece).wait_recv()

            for block in range(blocks):
                wide = hid[parity, block].astype(jnp.float32)
                square = jnp.sum(wide * wide, axis=-1, keepdims=True)
                if block < chips:
                    squares = squares + square
                else:
                    tail_squares = tail_squares + square
        tail_squares = jnp.broadcast_to(tail_squares, (TILE, HEAD_DIM))
        tail_squares = (tail_squares + turn(tail_squares))[:, :1]
        scale = lax.rsqrt(squares / (tensors * width) + NORM_EPSILON)
        tail_scale = lax.rsqrt(tail_squares / (tensors * width) + NORM_EPSILON)
        for parity in range(2):
            for pair in range(chips // 2):
                columns = [
                    slice((2 * at + parity) * width, (2 * at + parity + 1) * width)
                    for at in (2 * pair, 2 * pair + 1)
                ]
                gains = [jnp.broadcast_to(gain[:, at], (TILE, width)) for at in columns]
                tail = hid[parity, chips + pair].astype(jnp.float32)
                tail = tail * tail_scale * jnp.where(upper, gains[0], gains[1])
                for side, at in enumerate(columns):
                    wide = hid[parity, 2 * pair + side].astype(jnp.float32)
                    wide = wide * scale * gains[side]
                    both = jnp.concatenate([wide, tail if side == 0 else turn(tail)], axis=0)
                    normed[:, at] = both.astype(jnp.bfloat16)

        entered = normed[...]
        key_new = jnp.dot(entered, wk[...], preferred_element_type=jnp.float32)
        value_new = jnp.dot(entered, wv[...], preferred_element_type=jnp.float32)
        tail_values[batch] = value_new[TILE:, :]
        value_new = value_new.astype(jnp.bfloat16)
        main_rows = slice(batch * TILE, (batch + 1) * TILE)
        out_values[0, main_rows, :] = value_new[:TILE, :]
        keys = []
        values = []
        for kv in range(kv_local):
            at = slice(kv * HEAD_DIM, (kv + 1) * HEAD_DIM)
            rotated = rotate(key_new[:, at])
            tail_keys[batch, :, at] = rotated[TILE:, :]
            rotated = rotated.astype(jnp.bfloat16)
            out_keys[0, main_rows, at] = rotated[:TILE, :]
            keys.append(rotated.astype(jnp.float32))
            values.append(value_new[:, at].astype(jnp.float32))

        tile = min(256, heads * HEAD_DIM)
        for start in range(0, heads * HEAD_DIM, tile):
            product = jnp.dot(
                entered, wq[:, start : start + tile], preferred_element_type=jnp.float32
            )
            for side in range(tile // HEAD_DIM):
                head = start // HEAD_DIM + side
                kv = head // groups_per_kv
                query = rotate(product[:, side * HEAD_DIM : (side + 1) * HEAD_DIM])
                query = query.astype(jnp.bfloat16).astype(jnp.float32)
                at = pl.ds(first_line + head, PADDED, stride=slot)
                queries[at, :] = query
                score = jnp.sum(query * keys[kv], axis=-1, keepdims=True) * inv_root
                score_new[at, :] = jnp.broadcast_to(score, (PADDED, HEAD_DIM))
                values_new[at, :] = values[kv]

        for index in range(live):
            at = slice(first_line + index * slot, first_line + (index + 1) * slot)
            query = queries[at, :]
            spread = jnp.concatenate(
                [jnp.where(head_of == kv, query, 0.0) for kv in range(kv_local)], axis=1
            ).astype(jnp.bfloat16)
            scores[at, :] = lax.dot_general(
                spread, kc[row_of(batch, index)], (((1,), (1,)), ((), ())),
                preferred_element_type=jnp.float32,
            )

        lines = slice(first_line, first_line + live * slot)
        old = jnp.where(mask[lines, :] > 0.0, scores[lines, :] * inv_root, MASKED_SCORE)
        new = score_new[lines, :1]
        highest = jnp.maximum(jnp.max(old, axis=-1, keepdims=True), new)
        weight_old = jnp.exp(old - highest)
        weight_new = jnp.exp(new - highest)
        denominator = jnp.sum(weight_old, axis=-1, keepdims=True) + weight_new
        scores[lines, :] = weight_old / denominator
        weight_new = (weight_new / denominator).astype(jnp.bfloat16).astype(jnp.float32)
        values_new[lines, :] = values_new[lines, :] * weight_new

        for index in range(live):
            at = slice(first_line + index * slot, first_line + (index + 1) * slot)
            mixed = jnp.dot(
                scores[at, :].astype(jnp.bfloat16), vc[row_of(batch, index)],
                preferred_element_type=jnp.float32,
            )
            taken = mixed[:, :HEAD_DIM]
            for kv in range(1, kv_local):
                taken = jnp.where(
                    head_of == kv, mixed[:, kv * HEAD_DIM : (kv + 1) * HEAD_DIM], taken
                )
            attended[at, :] = taken + values_new[at, :]

        flat = jnp.concatenate(
            [
                attended[pl.ds(first_line + head, PADDED, stride=slot), :].astype(jnp.bfloat16)
                for head in range(heads)
            ],
            axis=1,
        )

        if batch == 0:
            @pl.when(section == 0)
            def _():
                loads["wo"].wait()

            @pl.when((section == 0) & inner)
            def _():
                pl.semaphore_wait(barrier, chips)

        @pl.when(inner)
        def _():
            send_before(stage).start()

        def project(order):
            parity, at = (1 - core, order) if order < chips else (core, order - chips)
            start = jnp.where(last, closing[order], 2 * at + parity) * width
            columns = pl.ds(pl.multiple_of(start, width), width)
            return jnp.dot(flat, wo[:, columns], preferred_element_type=jnp.float32)

        part, part_in, chip_sum = stage["part"], stage["part_in"], stage["chip_sum"]
        direct = stage["direct"]
        tail = None
        for order in range(chips):
            product = project(order)
            part[order] = product[:TILE, :].astype(jnp.bfloat16)
            if order % 2 == 0:
                tail = product[TILE:, :]
            else:
                part[chips + order // 2] = pack(tail, product[TILE:, :]).astype(jnp.bfloat16)

            @pl.when(last)
            def _():
                direct[order] = product.astype(jnp.bfloat16)
                send_direct(stage, order).start()

            if order + 1 in (chips // 2, chips):
                @pl.when(inner)
                def _():
                    send_part(stage, 0 if order + 1 < chips else 1).start()

        def add_up(piece, mine):
            first, end = pieces[piece]
            send_part(stage, piece).wait_recv()
            for block in range(first, end):
                if block < chips:
                    own_sum = mine[block][:TILE, :]
                else:
                    pair = 2 * (block - chips)
                    own_sum = pack(mine[pair][TILE:, :], mine[pair + 1][TILE:, :])
                chip_sum[block] = (
                    own_sum + part_in[block].astype(jnp.float32)
                ).astype(jnp.bfloat16)
            for step in range(1, chips + 1):
                send_sum(stage, lax.rem(chip + step, chips), piece).start()

        mine = [project(order) for order in range(chips, chips + chips // 2)]

        @pl.when(last)
        def _():
            for order in range(chips, chips + chips // 2):
                direct[order] = mine[order - chips].astype(jnp.bfloat16)
                send_direct(stage, order).start()

        @pl.when(inner)
        def _():
            add_up(0, mine)

        mine += [project(order) for order in range(chips + chips // 2, tensors)]

        @pl.when(last)
        def _():
            for order in range(chips + chips // 2, tensors - 1):
                direct[order] = mine[order - chips].astype(jnp.bfloat16)
                send_direct(stage, order).start()
            final[batch] = mine[-1]

        @pl.when(inner)
        def _():
            add_up(1, mine)

    def hand_over():
        for stage in stages:
            for at in range(chips):
                @pl.when(inner & (chip != at))
                def _():
                    for which in range(2):
                        send_owned(stage, at, which).start()

    odd = lax.rem(chip, 2) == 1

    def finish(batch):
        stage = stages[batch]

        @pl.when(last)
        def _():
            total = final[batch]
            for off in range(1, tensors):
                other = lax.rem(me + off, tensors)
                arrived = stage["direct_in"].at[other]
                remote(
                    arrived, arrived, stage["direct_send"].at[off - 1],
                    stage["direct_recv"].at[other], sibling,
                ).wait_recv()
                total = total + arrived[...].astype(jnp.float32)
            final[batch] = total

        @pl.when(inner)
        def _():
            owned_in, chip_sum = stage["owned_in"], stage["chip_sum"]
            owned_in[chip, 0] = chip_sum[chip]
            owned_in[chip, 1] = chip_sum[chips + chip // 2]
            totals = [jnp.zeros((TILE, width), jnp.float32) for _ in range(2)]
            for source in range(chips):
                @pl.when(chip != source)
                def _():
                    for which in range(2):
                        arrived = owned_in.at[source, which]
                        remote(
                            arrived, arrived, stage["owned_send"].at[source, which],
                            stage["owned_recv"].at[source, which], sibling,
                        ).wait_recv()

                for which in range(2):
                    totals[which] = totals[which] + owned_in[source, which].astype(jnp.float32)
            final[batch, :TILE, :] = totals[0]
            final[batch, TILE:, :] = jnp.where(odd, turn(totals[1]), totals[1])

        hid = stage["hid"]
        wide = hid[core, chip].astype(jnp.float32)
        main_on = running[0, batch, :TILE, :1]
        main = wide + main_on * final[batch, :TILE, :]
        out_hidden[0, batch * TILE : (batch + 1) * TILE, :] = main.astype(jnp.bfloat16)
        wide = hid[core, chips + chip // 2].astype(jnp.float32)
        wide = jnp.where(odd, turn(wide), wide)
        return wide + running[0, batch, TILE:, :1] * final[batch, TILE:, :]

    for batch in batches:
        take_entering(batch)
    for name in ("gain", "wk", "wv", "wq", "kc", "vc"):
        loads[name].wait()

    @pl.when(section > 0)
    def _():
        loads["wo"].wait()

    @pl.when((section > 0) & inner)
    def _():
        pl.semaphore_wait(barrier, chips)

    for batch in batches:
        receive(batch)
        compute(batch)
    hand_over()
    tails = slice(2 * TILE, 3 * TILE)
    for target, held in ((out_keys, tail_keys), (out_values, tail_values)):
        columns = held.shape[2]
        for start in range(0, columns, min(columns, width)):
            at = slice(start, start + min(columns, width))
            packed = pack(held[0, :, at], held[1, :, at])
            target[0, tails, at] = packed.astype(jnp.bfloat16)
    out_hidden[0, tails, :] = pack(finish(0), finish(1)).astype(jnp.bfloat16)

    for stage in stages:
        @pl.when(section == 0)
        def _():
            for off in range(1, tensors):
                entering(stage, off).wait_send()

        @pl.when(section > 0)
        def _():
            for piece in range(len(pieces)):
                swap_half(stage, core, piece).wait_send()

        @pl.when(last)
        def _():
            for order in range(tensors - 1):
                send_direct(stage, order).wait_send()

        @pl.when(inner)
        def _():
            send_before(stage).wait_send()
            for piece in range(len(pieces)):
                send_part(stage, piece).wait_send()
                for target in range(chips):
                    send_sum(stage, target, piece).wait_send()
            for at in range(chips):
                @pl.when(chip != at)
                def _():
                    for which in range(2):
                        send_owned(stage, at, which).wait_send()


def emit_kernel(hidden_ref, keys_ref, values_ref, out_hidden, out_keys, out_values):
    out_hidden[...] = hidden_ref[...]
    out_keys[...] = keys_ref[...]
    out_values[...] = values_ref[...]


def solution(mesh):
    sections = mesh.shape["section"]
    tensors = mesh.shape["tensor"]
    chips = tensors // 2

    def per_device(
        inputs, gains, w_query, w_key, w_value, w_out, key_cache, value_cache, cache_lens, exit_plan
    ):
        rows, width = inputs.shape
        features = gains.shape[1]
        query_width = w_query.shape[2]
        kv_width = w_key.shape[2]
        heads = query_width // HEAD_DIM
        groups_per_kv = query_width // kv_width
        slot = -(-heads // 8) * 8
        slots = key_cache.shape[2]
        any_spec = pl.BlockSpec(memory_space=pl.ANY)
        vmem_spec = pl.BlockSpec(memory_space=pltpu.VMEM)
        bf16, f32 = jnp.bfloat16, jnp.float32
        batches = 2
        lines = batches * PADDED * slot
        blocks = chips + chips // 2

        def stage_scratch(batch):
            def vmem(*shape):
                return pltpu.VMEM((*shape, width), bf16)

            def sems(*shape):
                return pltpu.SemaphoreType.DMA(shape)

            return dict(
                enter=vmem(2, chips, PADDED if batch == 0 else TILE),
                hid=vmem(2, blocks, TILE), before=vmem(blocks, TILE), part=vmem(blocks, TILE),
                part_in=vmem(blocks, TILE), chip_sum=vmem(blocks, TILE),
                sums_in=vmem(chips, blocks, TILE), owned_in=vmem(chips, 2, TILE),
                direct=vmem(tensors - 1, PADDED), direct_in=vmem(tensors, PADDED),
                enter_send=sems(tensors), enter_recv=sems(2, chips),
                half_send=sems(2), half_recv=sems(2), before_send=sems(1),
                before_recv=sems(1), part_send=sems(2), part_recv=sems(2),
                sums_send=sems(chips, 2), sums_recv=sems(chips, 2),
                owned_send=sems(chips, 2), owned_recv=sems(chips, 2),
                direct_send=sems(tensors - 1), direct_recv=sems(tensors),
            )

        results = pl.pallas_call(
            functools.partial(relay_kernel, sections, tensors, groups_per_kv),
            out_shape=(
                jax.ShapeDtypeStruct((1, rows, width), bf16),
                jax.ShapeDtypeStruct((1, rows, kv_width), bf16),
                jax.ShapeDtypeStruct((1, rows, kv_width), bf16),
            ),
            in_specs=[any_spec] * 10,
            out_specs=(vmem_spec,) * 3,
            scratch_shapes=[
                pltpu.VMEM((features, query_width), bf16),
                pltpu.VMEM((features, kv_width), bf16),
                pltpu.VMEM((features, kv_width), bf16),
                pltpu.VMEM((query_width, features), bf16),
                pltpu.VMEM((rows, slots, kv_width), bf16),
                pltpu.VMEM((rows, slots, kv_width), bf16),
                pltpu.VMEM((1, features), f32),
                pltpu.VMEM((rows, width), bf16),
                pltpu.VMEM((PADDED, features), bf16),
                pltpu.VMEM((batches, PADDED, HEAD_DIM), f32),
                pltpu.VMEM((2, batches, PADDED, HEAD_DIM), f32),
                pltpu.VMEM((lines, slots), f32),
                pltpu.VMEM((lines, HEAD_DIM), f32),
                pltpu.VMEM((lines, slots), f32),
                pltpu.VMEM((lines, HEAD_DIM), f32),
                pltpu.VMEM((lines, HEAD_DIM), f32),
                pltpu.VMEM((lines, HEAD_DIM), f32),
                pltpu.VMEM((batches, PADDED, width), f32),
                pltpu.VMEM((batches, TILE, kv_width), f32),
                pltpu.VMEM((batches, TILE, kv_width), f32),
                pltpu.SMEM((rows,), jnp.int32),
                pltpu.SMEM((rows,), jnp.int32),
                pltpu.SemaphoreType.DMA((10,)),
                tuple(stage_scratch(batch) for batch in range(batches)),
            ],
            compiler_params=pltpu.CompilerParams(
                collective_id=0, has_side_effects=True, vmem_limit_bytes=48 * 1024 * 1024
            ),
            name="relay",
        )(
            *(
                pltpu.with_memory_space_constraint(array, pltpu.HBM)
                for array in (
                    cache_lens, exit_plan, inputs, gains, w_query, w_key, w_value, w_out,
                    key_cache, value_cache,
                )
            )
        )
        return pl.pallas_call(
            emit_kernel,
            out_shape=tuple(jax.ShapeDtypeStruct(r.shape, r.dtype) for r in results),
            in_specs=[vmem_spec] * 3,
            out_specs=(vmem_spec,) * 3,
            compiler_params=pltpu.CompilerParams(vmem_limit_bytes=1024 * 1024),
            name="emit",
        )(*results)

    return jax.shard_map(
        per_device,
        mesh=mesh,
        in_specs=(
            P("group", "tensor"),
            P("section", None),
            P("section", None, "tensor"),
            P("section", None, "tensor"),
            P("section", None, "tensor"),
            P("section", "tensor", None),
            P("section", "group", None, "tensor"),
            P("section", "group", None, "tensor"),
            P("group"),
            P("group"),
        ),
        out_specs=(
            P("section", "group", "tensor"),
            P("section", "group", "tensor"),
            P("section", "group", "tensor"),
        ),
        check_vma=False,
    )
```
